512 devices in a mesh: blk: 64 (over x_hi, z, core), tgt: 8 (over y, x_lo).
Axes of the slice: x: 4 (x_hi: 2, x_lo: 2; x = x_hi * 2 + x_lo), y: 4, z: 16, core: 2. Of those that a mesh axis runs over, the one named last changes fastest.
Arguments:
- queries: bfloat16 [65536, 1024], P(('blk', 'tgt')), may hold values from -6 to 6
- keys: bfloat16 [4096, 1024], P('blk'), may hold values from -6 to 6
- values: bfloat16 [4096, 1024], P('blk'), may hold values from -6 to 6
- out_weight: bfloat16 [1024, 1024], P('tgt'), may hold values from -0.1875 to 0.1875
- out_grad: bfloat16 [65536, 1024], P(('blk', 'tgt')), may hold values from -24 to 24
Outputs:
- outputs: bfloat16 [65536, 1024], P(('blk', 'tgt'))
- query_grad: bfloat16 [65536, 1024], P(('blk', 'tgt'))
- key_grad: bfloat16 [4096, 1024], P('blk', 'tgt')
- value_grad: bfloat16 [4096, 1024], P('blk', 'tgt')
- weight_grad: bfloat16 [1024, 1024], P('tgt', 'blk')
The draws below stay inside these ranges and needn't reach their ends.
All inputs are finite; a program needn't handle non-finite values.
Results may differ from the reference program's by a relative error of at most 0.017.
Values may be sent and summed in bfloat16 or wider, within the bound.
No kernel may reach another device: no remote copies, remote signals or barrier semaphores. Data moves between devices by JAX's collectives and lax.ppermute only.
A program may use at most 64 MiB of HBM per device.

```python
import jax
import jax.numpy as jnp
from jax import lax

D = 1024
HEADS = 16
HD = 64
WIN = 5
TQ_DEV = 128
SRC_DEV = 64
QGROUP = 1024
TQ = 65536
SRC = 4096
N_TGT = 8


def draw_queries(key, part):
    drawn = jax.random.normal(jax.random.fold_in(key, 1), (TQ, D), jnp.float32)
    return jnp.clip(drawn, -6.0, 6.0).astype(jnp.bfloat16)


def draw_keys(key, part):
    drawn = jax.random.normal(jax.random.fold_in(key, 2), (SRC, D), jnp.float32)
    return jnp.clip(drawn, -6.0, 6.0).astype(jnp.bfloat16)


def with_spikes(drawn, rng, source, target, blocks, factor):
    def block_of(axis_at):
        return (jnp.arange(drawn.shape[axis_at]) // (drawn.shape[axis_at] // blocks)).reshape((-1,) + (1,) * (drawn.ndim - 1 - axis_at))

    first = jax.random.permutation(rng, blocks)[block_of(target)]
    far = (block_of(target) + blocks // 2) % blocks
    return jnp.where((block_of(source) == first) | (block_of(source) == far), factor * drawn, drawn)


def steps_of(rng, dims, cuts, smallest, top_value):
    factor_of, own = 1.0, jax.random.fold_in(rng, 6)
    for position, parts in cuts:
        steps = jnp.exp(jax.random.uniform(jax.random.fold_in(own, position), (parts,), jnp.float32, smallest / len(cuts), top_value / len(cuts)))
        factor_of = factor_of * jnp.repeat(steps, dims[position] // parts).reshape([-1 if axis == position else 1 for axis in range(len(dims))])
    return factor_of


def centred(rng, dims, deviation, reach, split=(), kind=jnp.bfloat16):
    array = deviation * jax.random.normal(rng, dims, jnp.float32)
    if split:
        array = array * steps_of(rng, dims, split, -0.22, 0.18)
    return jnp.clip(array, -reach, reach).astype(kind)


def gaussian_with(stream_key, extent, spread, limit, shards, heavy, kind=jnp.bfloat16):
    values = spread * jax.random.normal(stream_key, extent, jnp.float32)
    if shards:
        values = values * steps_of(stream_key, extent, shards, -0.22, 0.18)
    return jnp.clip(with_spikes(values, jax.random.fold_in(stream_key, 3), *heavy), -limit, limit).astype(kind)


def setup_inputs(seed: int = 0) -> dict:
    key_of = jax.random.split(jax.random.key(seed), 6)
    return {
        "queries": draw_queries(jax.random.fold_in(key_of[5], 71), 0),
        "keys": draw_keys(jax.random.fold_in(key_of[5], 71), 0),
        "values": centred(key_of[2], (SRC, D), 1.0, 6.0, ((0, 64),)),
        "out_weight": centred(key_of[3], (D, D), D ** -0.5, 0.1875, ((0, 8),)),
        "out_grad": gaussian_with(key_of[4], (TQ, D), 1.0, 24.0, ((0, 512),), (0, 1, 512, 6.0)),
    }


def attend_group(query_rows, key_rows, value_rows, grad_rows):
    scale = HD ** -0.5
    count = query_rows.shape[0]
    width = key_rows.shape[0]
    query_heads = query_rows.astype(jnp.float32).reshape(count, HEADS, HD)
    key_heads = key_rows.astype(jnp.float32).reshape(width, HEADS, HD)
    value_heads = value_rows.astype(jnp.float32).reshape(width, HEADS, HD)
    grad_heads = grad_rows.astype(jnp.float32).reshape(count, HEADS, HD)
    scores = jnp.einsum("rhd,jhd->hrj", query_heads, key_heads) * scale
    top = jnp.max(scores, axis=-1, keepdims=True)
    expo = jnp.exp(scores - top)
    probs = expo / jnp.sum(expo, axis=-1, keepdims=True)
    probs_low = probs.astype(jnp.bfloat16).astype(jnp.float32)
    attended = jnp.einsum("hrj,jhd->rhd", probs_low, value_heads).reshape(count, D).astype(jnp.bfloat16)
    prob_grad = jnp.einsum("rhd,jhd->hrj", grad_heads, value_heads)
    center = jnp.sum(probs * prob_grad, axis=-1, keepdims=True)
    score_grad = (scale * probs * (prob_grad - center)).astype(jnp.bfloat16).astype(jnp.float32)
    query_grad = jnp.einsum("hrj,jhd->rhd", score_grad, key_heads).reshape(count, D).astype(jnp.bfloat16)
    key_part = jnp.einsum("hrj,rhd->jhd", score_grad, query_heads).reshape(width, D)
    value_part = jnp.einsum("hrj,rhd->jhd", probs_low, grad_heads).reshape(width, D)
    return attended, query_grad, key_part, value_part


def reference(queries, keys, values, out_weight, out_grad):
    groups = SRC // SRC_DEV
    attended_grad = jnp.dot(out_grad, out_weight.T, preferred_element_type=jnp.float32).astype(jnp.bfloat16)

    def step(carry, index):
        key_grad, value_grad, weight_grad = carry
        start = (index * QGROUP).astype(jnp.int32)
        query_rows = lax.dynamic_slice_in_dim(queries, start, QGROUP, 0)
        grad_rows = lax.dynamic_slice_in_dim(attended_grad, start, QGROUP, 0)
        cot_rows = lax.dynamic_slice_in_dim(out_grad, start, QGROUP, 0)
        starts = [(((index - w) % groups) * SRC_DEV).astype(jnp.int32) for w in range(WIN)]
        key_rows = jnp.concatenate([lax.dynamic_slice_in_dim(keys, s, SRC_DEV, 0) for s in starts], axis=0)
        value_rows = jnp.concatenate([lax.dynamic_slice_in_dim(values, s, SRC_DEV, 0) for s in starts], axis=0)
        attended, query_grad, key_part, value_part = attend_group(query_rows, key_rows, value_rows, grad_rows)
        out_rows = jnp.dot(attended, out_weight, preferred_element_type=jnp.float32).astype(jnp.bfloat16)
        tiles_att = attended.astype(jnp.float32).reshape(N_TGT, TQ_DEV, D)
        tiles_cot = cot_rows.astype(jnp.float32).reshape(N_TGT, TQ_DEV, D)
        partial_value = jnp.einsum("trc,tre->tce", tiles_att, tiles_cot).astype(jnp.bfloat16).astype(jnp.float32)
        weight_grad = weight_grad + jnp.sum(partial_value, axis=0)
        for w in range(WIN):
            old_k = lax.dynamic_slice_in_dim(key_grad, starts[w], SRC_DEV, 0)
            key_grad = lax.dynamic_update_slice_in_dim(key_grad, old_k + key_part[w * SRC_DEV:(w + 1) * SRC_DEV], starts[w], 0)
            old_v = lax.dynamic_slice_in_dim(value_grad, starts[w], SRC_DEV, 0)
            value_grad = lax.dynamic_update_slice_in_dim(value_grad, old_v + value_part[w * SRC_DEV:(w + 1) * SRC_DEV], starts[w], 0)
        return (key_grad, value_grad, weight_grad), (out_rows, query_grad)

    init = (jnp.zeros((SRC, D), jnp.float32), jnp.zeros((SRC, D), jnp.float32), jnp.zeros((D, D), jnp.float32))
    (key_grad, value_grad, weight_grad), (out_all, query_all) = lax.scan(step, init, jnp.arange(groups, dtype=jnp.int32))
    outputs = out_all.reshape(TQ, D)
    query_grad = query_all.reshape(TQ, D)
    return outputs, query_grad, key_grad.astype(jnp.bfloat16), value_grad.astype(jnp.bfloat16), weight_grad.astype(jnp.bfloat16)
```

```python
import jax
import jax.numpy as jnp
from jax import lax
from jax.experimental import pallas as pl
from jax.experimental.pallas import tpu as pltpu
from jax.sharding import PartitionSpec as P

HD = 64
PAIR = 2 * HD
WIN = 5
SRC_DEV = 64
TILE = 256
F32 = jnp.float32
BF16 = jnp.bfloat16
NT = (((1,), (1,)), ((), ()))


def dot(a, b):
    return jnp.dot(a, b, preferred_element_type=F32)


def dot_nt(a, b):
    return lax.dot_general(a, b, NT, preferred_element_type=F32)


def attend_kernel(
    x_ref, own_ref, kv1_ref, kv2_ref, kv3_ref, kv4_ref, w_ref,
    back_ref, tile_ref, kv_own_ref, kv_send_ref,
    key_ref, value_ref, key_t_ref, value_t_ref, key_acc, value_acc, tile_acc,
):
    depth = w_ref.shape[1]
    width = WIN * SRC_DEV
    n_src, rows_src, _ = x_ref.shape
    lane = lax.broadcasted_iota(jnp.int32, (SRC_DEV, PAIR), 1)
    zero = jnp.zeros((SRC_DEV, PAIR), BF16)
    for w, ref in enumerate((own_ref, kv1_ref, kv2_ref, kv3_ref, kv4_ref)):
        block_key = ref[:, :PAIR]
        block_value = ref[:, PAIR:]
        for head in range(2):
            mine = (lane < HD) if head == 0 else (lane >= HD)
            at = pl.ds(head * width + w * SRC_DEV, SRC_DEV)
            key_ref[at, :] = jnp.where(mine, block_key, zero)
            value_ref[at, :] = jnp.where(mine, block_value, zero)
    key_t_ref[...] = key_ref[...].T
    value_t_ref[...] = value_ref[...].T
    scale = HD ** -0.5
    per_tile = TILE // rows_src
    steps = n_src // per_tile
    for step in range(steps):
        src = pl.ds(step * per_tile, per_tile)
        out_grad = x_ref[src, :, :depth].reshape(TILE, depth)
        query = x_ref[src, :, depth:].reshape(TILE, PAIR)
        att_grad = dot_nt(out_grad, w_ref[...]).astype(BF16)
        scores = dot_nt(key_ref[...], query)
        prob_grad = dot_nt(value_ref[...], att_grad)
        probs_low = []
        score_grad = []
        for head in range(2):
            part = scores[head * width : (head + 1) * width]
            grad = prob_grad[head * width : (head + 1) * width]
            top = jnp.max(part, axis=0, keepdims=True)
            expo = jnp.exp((part - top) * scale)
            probs = expo * (1.0 / jnp.sum(expo, axis=0, keepdims=True))
            center = jnp.sum(probs * grad, axis=0, keepdims=True)
            probs_low.append(probs.astype(BF16))
            score_grad.append((scale * probs * (grad - center)).astype(BF16))
        probs_low = jnp.concatenate(probs_low, axis=0)
        score_grad = jnp.concatenate(score_grad, axis=0)
        attended_t = dot(value_t_ref[...], probs_low)
        query_grad_t = dot(key_t_ref[...], score_grad)
        back_ref[src, :, :PAIR] = attended_t.T.astype(BF16).reshape(per_tile, rows_src, PAIR)
        back_ref[src, :, PAIR:] = query_grad_t.T.astype(BF16).reshape(per_tile, rows_src, PAIR)
        key_part = dot(score_grad, query)
        value_part = dot(probs_low, att_grad)
        tile_part = dot(attended_t.astype(BF16), out_grad)
        if step == 0:
            key_acc[...] = key_part
            value_acc[...] = value_part
            tile_acc[...] = tile_part
        else:
            key_acc[...] += key_part
            value_acc[...] += value_part
            tile_acc[...] += tile_part
    for w in range(WIN):
        for at, acc in ((0, key_acc), (PAIR, value_acc)):
            first = acc[w * SRC_DEV : (w + 1) * SRC_DEV]
            second = acc[width + w * SRC_DEV : width + (w + 1) * SRC_DEV]
            grad = jnp.where(lane < HD, first, second)
            if w == 0:
                kv_own_ref[:, at : at + PAIR] = grad
            else:
                kv_send_ref[w - 1, :, at : at + PAIR] = grad.astype(BF16)
    tile_ref[...] = tile_acc[...].T.astype(BF16)


def attend(x, kvs, weight):
    n_src, rows_src, wide = x.shape
    depth = weight.shape[1]
    width = WIN * SRC_DEV
    vmem = pl.BlockSpec(memory_space=pltpu.VMEM)
    flops = 2 * n_src * rows_src * (6 * 2 * width * PAIR + 2 * depth * PAIR)
    return pl.pallas_call(
        attend_kernel,
        out_shape=(
            jax.ShapeDtypeStruct((n_src, rows_src, 2 * PAIR), BF16),
            jax.ShapeDtypeStruct((depth, PAIR), BF16),
            jax.ShapeDtypeStruct((SRC_DEV, 2 * PAIR), F32),
            jax.ShapeDtypeStruct((WIN - 1, SRC_DEV, 2 * PAIR), BF16),
        ),
        in_specs=[vmem] * 7,
        out_specs=(vmem,) * 4,
        scratch_shapes=[
            pltpu.VMEM((2 * width, PAIR), BF16),
            pltpu.VMEM((2 * width, PAIR), BF16),
            pltpu.VMEM((PAIR, 2 * width), BF16),
            pltpu.VMEM((PAIR, 2 * width), BF16),
            pltpu.VMEM((2 * width, PAIR), F32),
            pltpu.VMEM((2 * width, PAIR), F32),
            pltpu.VMEM((PAIR, depth), F32),
        ],
        cost_estimate=pl.CostEstimate(
            flops=flops, bytes_accessed=2 * n_src * rows_src * wide, transcendentals=2 * width * n_src * rows_src
        ),
        compiler_params=pltpu.CompilerParams(vmem_limit_bytes=40 * 1024 * 1024),
        name="attend",
    )(x, *kvs, weight)


def project_kernel(odd_ref, back_ref, mine_ref, theirs_ref, out_ref, query_grad_ref):
    n_src, rows_src, _ = back_ref.shape
    depth = mine_ref.shape[2]
    odd = odd_ref[0] == 1
    total = jnp.zeros((rows_src, depth), F32)
    for src in range(0, n_src, 2):
        attended, weight = [], []
        for at in (src, src + 1):
            query_grad_ref[:, at * PAIR : (at + 1) * PAIR] = back_ref[at, :, PAIR:]
            part = back_ref[at, :, :PAIR].astype(F32)
            attended.append(jnp.where(odd, pltpu.roll(part, HD, 1), part).astype(BF16))
            weight += [mine_ref[at], theirs_ref[at]]
        total = total + dot(jnp.concatenate(attended, axis=1), jnp.concatenate(weight, axis=0))
    out_ref[...] = total.astype(BF16)


def project(odd, back, mine, theirs):
    n_src, rows_src, _ = back.shape
    depth = mine.shape[2]
    vmem = pl.BlockSpec(memory_space=pltpu.VMEM)
    out = jax.ShapeDtypeStruct((rows_src, depth), BF16)
    return pl.pallas_call(
        project_kernel,
        out_shape=(out, out),
        in_specs=[pl.BlockSpec(memory_space=pltpu.SMEM)] + [vmem] * 3,
        out_specs=(vmem, vmem),
        cost_estimate=pl.CostEstimate(
            flops=2 * rows_src * depth * depth, bytes_accessed=2 * depth * depth, transcendentals=0
        ),
        name="project",
    )(odd, back, mine, theirs)


def shift(value, axis, steps):
    count = lax.axis_size(axis)
    return lax.ppermute(value, axis, [(i, (i + steps) % count) for i in range(count)])


def partner(value, axis):
    return lax.ppermute(value, axis, [(i, i ^ 1) for i in range(lax.axis_size(axis))])


def swap(value, axis):
    return lax.all_to_all(value, axis, split_axis=0, concat_axis=0, tiled=True)


def local(queries, keys, values, out_weight, out_grad):
    n_tgt = lax.axis_size("tgt")
    n_blk = lax.axis_size("blk")
    rows, depth = queries.shape
    tgt = lax.axis_index("tgt")
    odd = lax.axis_index("blk") % 2
    own = jnp.concatenate(
        [lax.dynamic_slice_in_dim(a, tgt * PAIR, PAIR, 1) for a in (keys, values)], axis=1
    )
    kvs = [own] + [shift(own, "blk", w) for w in range(1, WIN)]
    wide = jnp.broadcast_to(out_grad[None], (n_tgt, rows, depth))
    split = queries.reshape(rows, n_tgt, PAIR).transpose(1, 0, 2)
    x = swap(jnp.concatenate([wide, split], axis=2), "tgt")
    half_rows = out_weight.shape[0] // 2
    half = lax.dynamic_slice_in_dim(out_weight, odd * half_rows, half_rows, 0)
    mine = swap(jnp.broadcast_to(half[None], (n_tgt, half_rows, depth)), "tgt")
    theirs = partner(mine, "blk")
    back, tile, kv_own, kv_send = attend(x, kvs, out_weight)
    back = swap(back, "tgt")
    tiles = swap(tile.reshape(n_blk, depth // n_blk, PAIR), "blk")
    weight_grad = jnp.sum(tiles.astype(F32), axis=0).T.astype(BF16)
    kv_grad = kv_own
    for w in range(1, WIN):
        kv_grad = kv_grad + shift(kv_send[w - 1], "blk", -w).astype(F32)
    kv_grad = kv_grad.astype(BF16)
    outputs, query_grad = project(odd.reshape(1), back, mine, theirs)
    return outputs, query_grad, kv_grad[:, :PAIR], kv_grad[:, PAIR:], weight_grad


def solution(mesh):
    return jax.shard_map(
        local,
        mesh=mesh,
        in_specs=(
            P(("blk", "tgt"), None),
            P("blk", None),
            P("blk", None),
            P("tgt", None),
            P(("blk", "tgt"), None),
        ),
        out_specs=(
            P(("blk", "tgt"), None),
            P(("blk", "tgt"), None),
            P("blk", "tgt"),
            P("blk", "tgt"),
            P("tgt", "blk"),
        ),
        check_vma=False,
    )
```

```python
import functools

import jax
import jax.numpy as jnp
from jax import lax
from jax.experimental import pallas as pl
from jax.experimental.pallas import tpu as pltpu
from jax.sharding import PartitionSpec as P


HD = 64
PAIR = 2 * HD
QUAD = 2 * PAIR
WIN = 5
SRC_DEV = 64
WIDTH = WIN * SRC_DEV
SCALE = HD ** -0.5
N_Y = 4
F32 = jnp.float32
BF16 = jnp.bfloat16
NT = (((1,), (1,)), ((), ()))
VMEM = pl.BlockSpec(memory_space=pltpu.VMEM)
SMEM = pl.BlockSpec(memory_space=pltpu.SMEM)


def dot(a, b):
    return jnp.dot(a, b, preferred_element_type=F32)


def dot_nt(a, b):
    return lax.dot_general(a, b, NT, preferred_element_type=F32)


def struct(shape, dtype=BF16):
    return jax.ShapeDtypeStruct(shape, dtype)


def pack_kernel(tgt_ref, query_ref, key_ref, value_ref, out_grad_ref, own_ref, send_ref):
    depth = out_grad_ref.shape[1]
    mine = pl.ds(pl.multiple_of((tgt_ref[0] >> 1) * QUAD, QUAD), QUAD)
    own_ref[:, :QUAD] = key_ref[:, mine]
    own_ref[:, QUAD:] = value_ref[:, mine]
    for i in range(N_Y):
        send_ref[i, :, :depth] = out_grad_ref[...]
        send_ref[i, :, depth:] = query_ref[:, i * QUAD : (i + 1) * QUAD]


def pack(tgt, queries, keys, values, out_grad):
    rows, depth = queries.shape
    return pl.pallas_call(
        pack_kernel,
        out_shape=(struct((SRC_DEV, 2 * QUAD)), struct((N_Y, rows, depth + QUAD))),
        in_specs=[SMEM] + [VMEM] * 4,
        out_specs=(VMEM,) * 2,
        compiler_params=pltpu.CompilerParams(vmem_limit_bytes=60 * 1024 * 1024),
        name="pack",
    )(tgt, queries, keys, values, out_grad)


def attend_kernel(
    chunk, tgt_ref, blk_ref, x_ref, own_ref, kv1_ref, kv2_ref, kv3_ref, kv4_ref, mine_ref, theirs_ref,
    back0, back1, back2, back3, four_ref,
    key_ref, value_ref, key_t_ref, value_t_ref, weight_ref, key_acc, value_acc, tile_acc,
):
    depth = mine_ref.shape[1]
    y = tgt_ref[0] >> 1
    low = tgt_ref[0] & 1
    lane = lax.broadcasted_iota(jnp.int32, (SRC_DEV, PAIR), 1)
    zero = jnp.zeros((SRC_DEV, PAIR), BF16)
    weight_ref[pl.ds(pl.multiple_of(low * PAIR, PAIR), PAIR), :] = mine_ref[...]
    weight_ref[pl.ds(pl.multiple_of((1 - low) * PAIR, PAIR), PAIR), :] = theirs_ref[...]
    for pair in range(2):
        for w, ref in enumerate((own_ref, kv1_ref, kv2_ref, kv3_ref, kv4_ref)):
            block_key = ref[:, pair * PAIR : (pair + 1) * PAIR]
            block_value = ref[:, QUAD + pair * PAIR : QUAD + (pair + 1) * PAIR]
            for head in range(2):
                own_lanes = (lane < HD) if head == 0 else (lane >= HD)
                at = pl.ds(head * WIDTH + w * SRC_DEV, SRC_DEV)
                key_ref[pair, at, :] = jnp.where(own_lanes, block_key, zero)
                value_ref[pair, at, :] = jnp.where(own_lanes, block_value, zero)
        key_t_ref[pair] = key_ref[pair].T
        value_t_ref[pair] = value_ref[pair].T
    backs = (back0, back1, back2, back3)
    rows = x_ref.shape[1]
    for step in range(N_Y // 2):
        here = (2 * step, 2 * step + 1)
        out_grad = jnp.concatenate([x_ref[y ^ s, :, :depth] for s in here], axis=0)
        att_grad_all = dot_nt(out_grad, weight_ref[...]).astype(BF16)
        attended, query_grad = [], []
        for pair in range(2):
            columns = slice(depth + pair * PAIR, depth + (pair + 1) * PAIR)
            query = jnp.concatenate([x_ref[y ^ s, :, columns] for s in here], axis=0)
            att_grad = att_grad_all[:, pair * PAIR : (pair + 1) * PAIR]
            scores = dot_nt(key_ref[pair], query)
            prob_grad = dot_nt(value_ref[pair], att_grad)
            probs_low, score_grad = [], []
            for head in range(2):
                part = scores[head * WIDTH : (head + 1) * WIDTH]
                grad = prob_grad[head * WIDTH : (head + 1) * WIDTH]
                top = jnp.max(part, axis=0, keepdims=True)
                expo = jnp.exp((part - top) * SCALE)
                probs = expo * (1.0 / jnp.sum(expo, axis=0, keepdims=True))
                center = jnp.sum(probs * grad, axis=0, keepdims=True)
                probs_low.append(probs.astype(BF16))
                score_grad.append((SCALE * probs * (grad - center)).astype(BF16))
            probs_low = jnp.concatenate(probs_low, axis=0)
            score_grad = jnp.concatenate(score_grad, axis=0)
            attended.append(dot(value_t_ref[pair], probs_low).astype(BF16))
            query_grad.append(dot(key_t_ref[pair], score_grad).astype(BF16))
            key_part = dot(score_grad, query)
            value_part = dot(probs_low, att_grad)
            if step == 0:
                key_acc[pair] = key_part
                value_acc[pair] = value_part
            else:
                key_acc[pair] += key_part
                value_acc[pair] += value_part
        attended = jnp.concatenate(attended, axis=0)
        query_grad = jnp.concatenate(query_grad, axis=0).T
        out_part = dot(attended.T, weight_ref[...]).astype(BF16)
        for k, i in enumerate(here):
            backs[i][:, :depth] = out_part[k * rows : (k + 1) * rows]
            backs[i][:, depth:] = query_grad[k * rows : (k + 1) * rows]
        tile_part = dot(attended, out_grad)
        if step == 0:
            tile_acc[...] = tile_part
        else:
            tile_acc[...] += tile_part
    core = blk_ref[0] & 1
    rows_tile = depth // 2
    for half in range(2):
        turned = tile_acc[half * PAIR : (half + 1) * PAIR, :].T.reshape(-1, 2, chunk, PAIR)
        for to in range(2):
            four_ref[2 * to + half, :rows_tile, :] = turned[:, to].reshape(rows_tile, PAIR).astype(BF16)
        for other in range(2):
            to = 2 * (core ^ other) + half
            for slot in range(WIN // 2 + 1):
                w = 2 * slot + other
                for part, acc in enumerate((key_acc, value_acc)):
                    at = pl.ds(rows_tile + (2 * slot + part) * SRC_DEV, SRC_DEV)
                    if w >= WIN:
                        four_ref[to, at, :] = zero
                        continue
                    first = acc[half, w * SRC_DEV : (w + 1) * SRC_DEV, :]
                    second = acc[half, WIDTH + w * SRC_DEV : WIDTH + (w + 1) * SRC_DEV, :]
                    four_ref[to, at, :] = jnp.where(lane < HD, first, second).astype(BF16)


def attend(tgt, blk, n_blk, x, kvs, mine, theirs):
    _, rows, wide = x.shape
    depth = mine.shape[1]
    flops = 2 * N_Y * rows * (6 * 2 * WIDTH * QUAD + 3 * depth * QUAD)
    return pl.pallas_call(
        functools.partial(attend_kernel, depth // n_blk),
        out_shape=(struct((rows, wide)),) * N_Y
        + (struct((4, depth // 2 + 2 * (WIN // 2 + 1) * SRC_DEV, PAIR)),),
        in_specs=[SMEM] * 2 + [VMEM] * 8,
        out_specs=(VMEM,) * (N_Y + 1),
        scratch_shapes=[
            pltpu.VMEM((2, 2 * WIDTH, PAIR), BF16),
            pltpu.VMEM((2, 2 * WIDTH, PAIR), BF16),
            pltpu.VMEM((2, PAIR, 2 * WIDTH), BF16),
            pltpu.VMEM((2, PAIR, 2 * WIDTH), BF16),
            pltpu.VMEM((QUAD, depth), BF16),
            pltpu.VMEM((2, 2 * WIDTH, PAIR), F32),
            pltpu.VMEM((2, 2 * WIDTH, PAIR), F32),
            pltpu.VMEM((QUAD, depth), F32),
        ],
        cost_estimate=pl.CostEstimate(
            flops=flops, bytes_accessed=4 * N_Y * rows * wide, transcendentals=4 * WIDTH * N_Y * rows
        ),
        compiler_params=pltpu.CompilerParams(vmem_limit_bytes=60 * 1024 * 1024),
        name="attend",
    )(tgt, blk, x, *kvs, mine, theirs)


def combine_kernel(blk_ref, four_ref, tile_ref, own_ref, near_ref, far_ref):
    chips, chunk, _ = tile_ref.shape
    rows_tile = chips * chunk
    block = 2 * SRC_DEV
    core = blk_ref[0] & 1
    total = four_ref[0, :rows_tile, :].astype(F32)
    for i in range(1, 4):
        total = total + four_ref[i, :rows_tile, :].astype(F32)
    tile_ref[...] = total.astype(BF16).reshape(chips, chunk, PAIR)

    def part(of_core, slot):
        at = pl.ds(rows_tile + slot * block, block)
        return four_ref[2 * of_core, at, :].astype(F32) + four_ref[2 * of_core + 1, at, :].astype(F32)

    one, three = part(1 - core, 0), part(1 - core, 1)
    zero = jnp.zeros_like(one)
    first = core == 0
    own_ref[...] = part(core, 0) + jnp.where(first, one, zero)
    near_ref[...] = (part(core, 1) + jnp.where(first, three, one)).astype(BF16)
    far_ref[...] = (part(core, 2) + jnp.where(first, zero, three)).astype(BF16)


def combine(blk, n_blk, four):
    rows_tile = four.shape[1] - 2 * (WIN // 2 + 1) * SRC_DEV
    chips = n_blk // 2
    block = (2 * SRC_DEV, PAIR)
    return pl.pallas_call(
        combine_kernel,
        out_shape=(struct((chips, rows_tile // chips, PAIR)), struct(block, F32), struct(block), struct(block)),
        in_specs=[SMEM, VMEM],
        out_specs=(VMEM,) * 4,
        compiler_params=pltpu.CompilerParams(vmem_limit_bytes=8 * 1024 * 1024),
        name="combine",
    )(blk, four)


def finish_kernel(tgt_ref, back0, back1, back2, back3, own_ref, near_ref, far_ref, out_ref, query_grad_ref, key_grad_ref, value_grad_ref):
    depth = out_ref.shape[1]
    total = None
    for s, ref in enumerate((back0, back1, back2, back3)):
        part = ref[:, :depth].astype(F32)
        total = part if total is None else total + part
        query_grad_ref[:, pl.ds(pl.multiple_of(((tgt_ref[0] >> 1) ^ s) * QUAD, QUAD), QUAD)] = ref[:, depth:]
    out_ref[...] = total.astype(BF16)
    grad = (own_ref[...] + near_ref[...].astype(F32) + far_ref[...].astype(F32)).astype(BF16)
    key_grad_ref[...] = grad[:SRC_DEV]
    value_grad_ref[...] = grad[SRC_DEV:]


def finish(tgt, backs, own, near, far):
    rows, wide = backs[0].shape
    out, grad = struct((rows, wide - QUAD)), struct((SRC_DEV, PAIR))
    return pl.pallas_call(
        finish_kernel,
        out_shape=(out, out, grad, grad),
        in_specs=[SMEM] + [VMEM] * (N_Y + 3),
        out_specs=(VMEM,) * 4,
        cost_estimate=pl.CostEstimate(
            flops=N_Y * rows * wide, bytes_accessed=2 * N_Y * rows * wide, transcendentals=0
        ),
        compiler_params=pltpu.CompilerParams(vmem_limit_bytes=8 * 1024 * 1024),
        name="finish",
    )(tgt, *backs, own, near, far)


def total_kernel(part_ref, total_ref):
    total = part_ref[0].astype(F32)
    for i in range(1, part_ref.shape[0]):
        total = total + part_ref[i].astype(F32)
    total_ref[...] = total.astype(BF16)


def total_of(parts):
    return pl.pallas_call(
        total_kernel,
        out_shape=struct(parts.shape[1:]),
        in_specs=[VMEM],
        out_specs=VMEM,
        compiler_params=pltpu.CompilerParams(vmem_limit_bytes=4 * 1024 * 1024),
        name="total",
    )(parts)


def shift(value, axis, steps):
    count = lax.axis_size(axis)
    return lax.ppermute(value, axis, [(i, (i + steps) % count) for i in range(count)])


def flip(value, bits):
    return lax.ppermute(value, "tgt", [(i, i ^ bits) for i in range(lax.axis_size("tgt"))])


def local(queries, keys, values, out_weight, out_grad):
    n_blk = lax.axis_size("blk")
    n_tgt = lax.axis_size("tgt")
    tgt = lax.axis_index("tgt").reshape(1)
    blk = lax.axis_index("blk").reshape(1)
    own, send = pack(tgt, queries, keys, values, out_grad)
    groups = [[2 * y + low for y in range(N_Y)] for low in range(2)]
    x = lax.all_to_all(
        send, "tgt", split_axis=0, concat_axis=0, tiled=True, axis_index_groups=groups
    )
    theirs = flip(out_weight, 1)
    kvs = [own] + [shift(own, "blk", w) for w in range(1, WIN)]
    *backs, four = attend(tgt, blk, n_blk, x, kvs, out_weight, theirs)
    fours = [
        [(2 * chip + core) * n_tgt + 2 * y + low for core in range(2) for low in range(2)]
        for chip in range(n_blk // 2)
        for y in range(N_Y)
    ]
    four = lax.all_to_all(four, ("blk", "tgt"), split_axis=0, concat_axis=0, tiled=True, axis_index_groups=fours)
    backs = [backs[0]] + [flip(backs[s], 2 * s) for s in range(1, N_Y)]
    tile, own_grad, near, far = combine(blk, n_blk, four)
    cores = [list(range(core, n_blk, 2)) for core in range(2)]
    tiles = lax.all_to_all(
        tile, "blk", split_axis=0, concat_axis=0, tiled=True, axis_index_groups=cores
    )
    near, far = shift(near, "blk", -2), shift(far, "blk", -4)
    outputs, query_grad, key_grad, value_grad = finish(tgt, backs, own_grad, near, far)
    weight_grad = total_of(tiles).T
    return outputs, query_grad, key_grad, value_grad, weight_grad


def solution(mesh):
    return jax.shard_map(
        local,
        mesh=mesh,
        in_specs=(
            P(("blk", "tgt"), None),
            P("blk", None),
            P("blk", None),
            P("tgt", None),
            P(("blk", "tgt"), None),
        ),
        out_specs=(
            P(("blk", "tgt"), None),
            P(("blk", "tgt"), None),
            P("blk", "tgt"),
            P("blk", "tgt"),
            P("tgt", "blk"),
        ),
        check_vma=False,
    )
```

```python
import functools

import jax
import jax.numpy as jnp
from jax import lax
from jax.experimental import pallas as pl
from jax.experimental.pallas import tpu as pltpu
from jax.sharding import PartitionSpec as P


HD = 64
PAIR = 2 * HD
QUAD = 2 * PAIR
WIN = 5
SRC_DEV = 64
WIDTH = WIN * SRC_DEV
SCALE = HD ** -0.5
N_Y = 4
F32 = jnp.float32
BF16 = jnp.bfloat16
NT = (((1,), (1,)), ((), ()))
VMEM = pl.BlockSpec(memory_space=pltpu.VMEM)
SMEM = pl.BlockSpec(memory_space=pltpu.SMEM)


def dot(a, b):
    return jnp.dot(a, b, preferred_element_type=F32)


def dot_nt(a, b):
    return lax.dot_general(a, b, NT, preferred_element_type=F32)


def struct(shape, dtype=BF16):
    return jax.ShapeDtypeStruct(shape, dtype)


def pack_kernel(tgt_ref, query_ref, key_ref, value_ref, out_grad_ref, own_ref, send_ref):
    depth = out_grad_ref.shape[1]
    mine = pl.ds(pl.multiple_of((tgt_ref[0] >> 1) * QUAD, QUAD), QUAD)
    own_ref[:, :QUAD] = key_ref[:, mine]
    own_ref[:, QUAD:] = value_ref[:, mine]
    for i in range(N_Y):
        send_ref[i, :, :depth] = out_grad_ref[...]
        send_ref[i, :, depth:] = query_ref[:, i * QUAD : (i + 1) * QUAD]


def pack(tgt, queries, keys, values, out_grad):
    rows, depth = queries.shape
    return pl.pallas_call(
        pack_kernel,
        out_shape=(struct((SRC_DEV, 2 * QUAD)), struct((N_Y, rows, depth + QUAD))),
        in_specs=[SMEM] + [VMEM] * 4,
        out_specs=(VMEM,) * 2,
        compiler_params=pltpu.CompilerParams(vmem_limit_bytes=60 * 1024 * 1024),
        name="pack",
    )(tgt, queries, keys, values, out_grad)


def attend_kernel(
    chunk, tgt_ref, x_ref, own_ref, kv1_ref, kv2_ref, kv3_ref, kv4_ref, mine_ref, theirs_ref,
    back0, back1, back2, back3, eight_ref, keep_ref, low_ref, core_ref, both_ref,
    key_ref, value_ref, key_t_ref, value_t_ref, weight_ref, key_acc, value_acc, tile_acc,
):
    depth = mine_ref.shape[1]
    y = tgt_ref[0] >> 1
    low = tgt_ref[0] & 1
    lane = lax.broadcasted_iota(jnp.int32, (SRC_DEV, PAIR), 1)
    zero = jnp.zeros((SRC_DEV, PAIR), BF16)
    weight_ref[pl.ds(pl.multiple_of(low * PAIR, PAIR), PAIR), :] = mine_ref[...]
    weight_ref[pl.ds(pl.multiple_of((1 - low) * PAIR, PAIR), PAIR), :] = theirs_ref[...]
    for pair in range(2):
        for w, ref in enumerate((own_ref, kv1_ref, kv2_ref, kv3_ref, kv4_ref)):
            block_key = ref[:, pair * PAIR : (pair + 1) * PAIR]
            block_value = ref[:, QUAD + pair * PAIR : QUAD + (pair + 1) * PAIR]
            for head in range(2):
                own_lanes = (lane < HD) if head == 0 else (lane >= HD)
                at = pl.ds(head * WIDTH + w * SRC_DEV, SRC_DEV)
                key_ref[pair, at, :] = jnp.where(own_lanes, block_key, zero)
                value_ref[pair, at, :] = jnp.where(own_lanes, block_value, zero)
        key_t_ref[pair] = key_ref[pair].T
        value_t_ref[pair] = value_ref[pair].T
    backs = (back0, back1, back2, back3)
    rows = x_ref.shape[1]
    for step in range(N_Y // 2):
        here = (2 * step, 2 * step + 1)
        out_grad = jnp.concatenate([x_ref[y ^ s, :, :depth] for s in here], axis=0)
        att_grad_all = dot_nt(out_grad, weight_ref[...]).astype(BF16)
        attended, query_grad = [], []
        for pair in range(2):
            columns = slice(depth + pair * PAIR, depth + (pair + 1) * PAIR)
            query = jnp.concatenate([x_ref[y ^ s, :, columns] for s in here], axis=0)
            att_grad = att_grad_all[:, pair * PAIR : (pair + 1) * PAIR]
            scores = dot_nt(key_ref[pair], query)
            prob_grad = dot_nt(value_ref[pair], att_grad)
            probs_low, score_grad = [], []
            for head in range(2):
                part = scores[head * WIDTH : (head + 1) * WIDTH]
                grad = prob_grad[head * WIDTH : (head + 1) * WIDTH]
                top = jnp.max(part, axis=0, keepdims=True)
                expo = jnp.exp((part - top) * SCALE)
                probs = expo * (1.0 / jnp.sum(expo, axis=0, keepdims=True))
                center = jnp.sum(probs * grad, axis=0, keepdims=True)
                probs_low.append(probs.astype(BF16))
                score_grad.append((SCALE * probs * (grad - center)).astype(BF16))
            probs_low = jnp.concatenate(probs_low, axis=0)
            score_grad = jnp.concatenate(score_grad, axis=0)
            attended.append(dot(value_t_ref[pair], probs_low).astype(BF16))
            query_grad.append(dot(key_t_ref[pair], score_grad).astype(BF16))
            key_part = dot(score_grad, query)
            value_part = dot(probs_low, att_grad)
            if step == 0:
                key_acc[pair] = key_part
                value_acc[pair] = value_part
            else:
                key_acc[pair] += key_part
                value_acc[pair] += value_part
        attended = jnp.concatenate(attended, axis=0)
        query_grad = jnp.concatenate(query_grad, axis=0).T
        out_part = dot(attended.T, weight_ref[...]).astype(BF16)
        for k, i in enumerate(here):
            backs[i][:, :depth] = out_part[k * rows : (k + 1) * rows]
            backs[i][:, depth:] = query_grad[k * rows : (k + 1) * rows]
        tile_part = dot(attended, out_grad)
        if step == 0:
            tile_acc[...] = tile_part
        else:
            tile_acc[...] += tile_part
    for half in range(2):
        turned = tile_acc[half * PAIR : (half + 1) * PAIR, :].T.reshape(2, -1, 2, chunk, PAIR)
        for high in range(2):
            for core in range(2):
                eight_ref[4 * high + 2 * core + half] = turned[high, :, core].astype(BF16)
    for pair, even, odd in ((low, keep_ref, core_ref), (1 - low, low_ref, both_ref)):
        for w in range(WIN):
            ref = odd if w % 2 else even
            for part, acc in enumerate((key_acc, value_acc)):
                first = acc[pair, w * SRC_DEV : (w + 1) * SRC_DEV, :]
                second = acc[pair, WIDTH + w * SRC_DEV : WIDTH + (w + 1) * SRC_DEV, :]
                at = slice(part * SRC_DEV, (part + 1) * SRC_DEV)
                ref[w // 2, at, :] = jnp.where(lane < HD, first, second).astype(ref.dtype)


def attend(tgt, n_blk, x, kvs, mine, theirs):
    _, rows, wide = x.shape
    depth = mine.shape[1]
    flops = 2 * N_Y * rows * (6 * 2 * WIDTH * QUAD + 3 * depth * QUAD)
    return pl.pallas_call(
        functools.partial(attend_kernel, depth // n_blk),
        out_shape=(struct((rows, wide)),) * N_Y
        + (
            struct((8, n_blk // 4, depth // n_blk, PAIR)),
            struct((3, 2 * SRC_DEV, PAIR), F32),
            struct((3, 2 * SRC_DEV, PAIR)),
            struct((2, 2 * SRC_DEV, PAIR)),
            struct((2, 2 * SRC_DEV, PAIR)),
        ),
        in_specs=[SMEM] + [VMEM] * 8,
        out_specs=(VMEM,) * (N_Y + 5),
        scratch_shapes=[
            pltpu.VMEM((2, 2 * WIDTH, PAIR), BF16),
            pltpu.VMEM((2, 2 * WIDTH, PAIR), BF16),
            pltpu.VMEM((2, PAIR, 2 * WIDTH), BF16),
            pltpu.VMEM((2, PAIR, 2 * WIDTH), BF16),
            pltpu.VMEM((QUAD, depth), BF16),
            pltpu.VMEM((2, 2 * WIDTH, PAIR), F32),
            pltpu.VMEM((2, 2 * WIDTH, PAIR), F32),
            pltpu.VMEM((QUAD, depth), F32),
        ],
        cost_estimate=pl.CostEstimate(
            flops=flops, bytes_accessed=4 * N_Y * rows * wide, transcendentals=4 * WIDTH * N_Y * rows
        ),
        compiler_params=pltpu.CompilerParams(vmem_limit_bytes=60 * 1024 * 1024),
        name="attend",
    )(tgt, x, *kvs, mine, theirs)


def combine_kernel(blk_ref, eight_ref, keep_ref, low_ref, core_ref, both_ref, tile_ref, own_ref, near_ref, far_ref):
    total = eight_ref[0].astype(F32)
    for i in range(1, eight_ref.shape[0]):
        total = total + eight_ref[i].astype(F32)
    tile_ref[...] = total.astype(BF16)

    def same(slot):
        return keep_ref[slot] + low_ref[slot].astype(F32)

    one, three = (core_ref[slot].astype(F32) + both_ref[slot].astype(F32) for slot in range(2))
    zero = jnp.zeros_like(one)
    first = (blk_ref[0] & 1) == 0
    own_ref[...] = same(0) + jnp.where(first, one, zero)
    near_ref[...] = (same(1) + jnp.where(first, three, one)).astype(BF16)
    far_ref[...] = (same(2) + jnp.where(first, zero, three)).astype(BF16)


def combine(blk, eight, *parts):
    block = (2 * SRC_DEV, PAIR)
    return pl.pallas_call(
        combine_kernel,
        out_shape=(struct(eight.shape[1:]), struct(block, F32), struct(block), struct(block)),
        in_specs=[SMEM] + [VMEM] * 5,
        out_specs=(VMEM,) * 4,
        compiler_params=pltpu.CompilerParams(vmem_limit_bytes=8 * 1024 * 1024),
        name="combine",
    )(blk, eight, *parts)


def finish_kernel(tgt_ref, back0, back1, back2, back3, own_ref, near_ref, far_ref, out_ref, query_grad_ref, key_grad_ref, value_grad_ref):
    depth = out_ref.shape[1]
    total = None
    for s, ref in enumerate((back0, back1, back2, back3)):
        part = ref[:, :depth].astype(F32)
        total = part if total is None else total + part
        query_grad_ref[:, pl.ds(pl.multiple_of(((tgt_ref[0] >> 1) ^ s) * QUAD, QUAD), QUAD)] = ref[:, depth:]
    out_ref[...] = total.astype(BF16)
    grad = (own_ref[...] + near_ref[...].astype(F32) + far_ref[...].astype(F32)).astype(BF16)
    key_grad_ref[...] = grad[:SRC_DEV]
    value_grad_ref[...] = grad[SRC_DEV:]


def finish(tgt, backs, own, near, far):
    rows, wide = backs[0].shape
    out, grad = struct((rows, wide - QUAD)), struct((SRC_DEV, PAIR))
    return pl.pallas_call(
        finish_kernel,
        out_shape=(out, out, grad, grad),
        in_specs=[SMEM] + [VMEM] * (N_Y + 3),
        out_specs=(VMEM,) * 4,
        cost_estimate=pl.CostEstimate(
            flops=N_Y * rows * wide, bytes_accessed=2 * N_Y * rows * wide, transcendentals=0
        ),
        compiler_params=pltpu.CompilerParams(vmem_limit_bytes=8 * 1024 * 1024),
        name="finish",
    )(tgt, *backs, own, near, far)


def total_kernel(part_ref, total_ref):
    total = part_ref[0].astype(F32)
    for i in range(1, part_ref.shape[0]):
        total = total + part_ref[i].astype(F32)
    total_ref[...] = total.astype(BF16)


def total_of(parts):
    return pl.pallas_call(
        total_kernel,
        out_shape=struct(parts.shape[1:]),
        in_specs=[VMEM],
        out_specs=VMEM,
        compiler_params=pltpu.CompilerParams(vmem_limit_bytes=4 * 1024 * 1024),
        name="total",
    )(parts)


def shift(value, axis, steps):
    count = lax.axis_size(axis)
    return lax.ppermute(value, axis, [(i, (i + steps) % count) for i in range(count)])


def flip(value, bits, blk_bits=0):
    n_tgt = lax.axis_size("tgt")
    devices = range(lax.axis_size("blk") * n_tgt)
    return lax.ppermute(value, ("blk", "tgt"), [(i, i ^ (blk_bits * n_tgt + bits)) for i in devices])


def local(queries, keys, values, out_weight, out_grad):
    n_blk = lax.axis_size("blk")
    n_tgt = lax.axis_size("tgt")
    tgt = lax.axis_index("tgt").reshape(1)
    blk = lax.axis_index("blk").reshape(1)
    own, send = pack(tgt, queries, keys, values, out_grad)
    groups = [[2 * y + low for y in range(N_Y)] for low in range(2)]
    x = lax.all_to_all(
        send, "tgt", split_axis=0, concat_axis=0, tiled=True, axis_index_groups=groups
    )
    theirs = flip(out_weight, 1)
    kvs = [own] + [shift(own, "blk", w) for w in range(1, WIN)]
    *backs, eight, keep, to_low, to_core, to_both = attend(tgt, n_blk, x, kvs, out_weight, theirs)
    n_z = n_blk // 4
    eights = [
        [((high * n_z + z) * 2 + core) * n_tgt + 2 * y + low for high in range(2) for core in range(2) for low in range(2)]
        for z in range(n_z)
        for y in range(N_Y)
    ]
    eight = lax.all_to_all(eight, ("blk", "tgt"), split_axis=0, concat_axis=0, tiled=True, axis_index_groups=eights)
    parts = [keep, flip(to_low, 1), flip(to_core, 0, 1), flip(to_both, 1, 1)]
    back2 = flip(backs[2], 4)
    backs = [backs[0], flip(backs[1], 2), back2, flip(backs[3], 6)]
    tile, own_grad, near, far = combine(blk, eight, *parts)
    lines = [[(high * n_z + z) * 2 + core for z in range(n_z)] for high in range(2) for core in range(2)]
    tiles = lax.all_to_all(
        tile, "blk", split_axis=0, concat_axis=0, tiled=True, axis_index_groups=lines
    )
    near, far = shift(near, "blk", -2), shift(far, "blk", -4)
    outputs, query_grad, key_grad, value_grad = finish(tgt, backs, own_grad, near, far)
    weight_grad = total_of(tiles).T
    return outputs, query_grad, key_grad, value_grad, weight_grad


def solution(mesh):
    return jax.shard_map(
        local,
        mesh=mesh,
        in_specs=(
            P(("blk", "tgt"), None),
            P("blk", None),
            P("blk", None),
            P("tgt", None),
            P(("blk", "tgt"), None),
        ),
        out_specs=(
            P(("blk", "tgt"), None),
            P(("blk", "tgt"), None),
            P("blk", "tgt"),
            P("blk", "tgt"),
            P("tgt", "blk"),
        ),
        check_vma=False,
    )
```

```python
import functools

import jax
import jax.numpy as jnp
from jax import lax
from jax.experimental import pallas as pl
from jax.experimental.pallas import tpu as pltpu
from jax.sharding import PartitionSpec as P


HD = 64
PAIR = 2 * HD
QUAD = 2 * PAIR
WIN = 5
SRC_DEV = 64
WIDTH = WIN * SRC_DEV
SCALE = HD ** -0.5
N_Y = 4
F32 = jnp.float32
BF16 = jnp.bfloat16
NT = (((1,), (1,)), ((), ()))
VMEM = pl.BlockSpec(memory_space=pltpu.VMEM)
SMEM = pl.BlockSpec(memory_space=pltpu.SMEM)


def dot(a, b):
    return jnp.dot(a, b, preferred_element_type=F32)


def dot_nt(a, b):
    return lax.dot_general(a, b, NT, preferred_element_type=F32)


def struct(shape, dtype=BF16):
    return jax.ShapeDtypeStruct(shape, dtype)


def pack_kernel(tgt_ref, query_ref, key_ref, value_ref, out_grad_ref, own_ref, send_ref):
    depth = out_grad_ref.shape[1]
    mine = pl.ds(pl.multiple_of((tgt_ref[0] >> 1) * QUAD, QUAD), QUAD)
    own_ref[:, :QUAD] = key_ref[:, mine]
    own_ref[:, QUAD:] = value_ref[:, mine]
    for i in range(N_Y):
        send_ref[i, :, :depth] = out_grad_ref[...]
        send_ref[i, :, depth:] = query_ref[:, i * QUAD : (i + 1) * QUAD]


def pack(tgt, queries, keys, values, out_grad):
    rows, depth = queries.shape
    return pl.pallas_call(
        pack_kernel,
        out_shape=(struct((SRC_DEV, 2 * QUAD)), struct((N_Y, rows, depth + QUAD))),
        in_specs=[SMEM] + [VMEM] * 4,
        out_specs=(VMEM,) * 2,
        compiler_params=pltpu.CompilerParams(vmem_limit_bytes=60 * 1024 * 1024),
        name="pack",
    )(tgt, queries, keys, values, out_grad)


def attend_kernel(
    chunk, tgt_ref, blk_ref, x_ref, own_ref, mate_ref, kept_ref, low_ref, core_ref, both_ref, mine_ref, theirs_ref,
    back0, back1, back2, back3, four_ref,
    key_ref, value_ref, key_t_ref, value_t_ref, weight_ref, key_acc, value_acc, tile_acc,
):
    depth = mine_ref.shape[1]
    y = tgt_ref[0] >> 1
    low = tgt_ref[0] & 1
    lane = lax.broadcasted_iota(jnp.int32, (SRC_DEV, PAIR), 1)
    zero = jnp.zeros((SRC_DEV, PAIR), BF16)
    weight_ref[pl.ds(pl.multiple_of(low * PAIR, PAIR), PAIR), :] = mine_ref[...]
    weight_ref[pl.ds(pl.multiple_of((1 - low) * PAIR, PAIR), PAIR), :] = theirs_ref[...]
    is_low, first = low == 0, (blk_ref[0] & 1) == 0
    kept, other_low, other_core, both = kept_ref[...], low_ref[...], core_ref[...], both_ref[...]
    near = jnp.where(is_low, other_core, both)
    blocks = (
        own_ref[...],
        jnp.where(first, near, mate_ref[...]),
        jnp.where(is_low, kept, other_low),
        jnp.where(first, jnp.where(is_low, both, other_core), near),
        jnp.where(is_low, other_low, kept),
    )
    for pair in range(2):
        for w, block in enumerate(blocks):
            block_key = block[:, pair * PAIR : (pair + 1) * PAIR]
            block_value = block[:, QUAD + pair * PAIR : QUAD + (pair + 1) * PAIR]
            for head in range(2):
                own_lanes = (lane < HD) if head == 0 else (lane >= HD)
                at = pl.ds(head * WIDTH + w * SRC_DEV, SRC_DEV)
                key_ref[pair, at, :] = jnp.where(own_lanes, block_key, zero)
                value_ref[pair, at, :] = jnp.where(own_lanes, block_value, zero)
        key_t_ref[pair] = key_ref[pair].T
        value_t_ref[pair] = value_ref[pair].T
    backs = (back0, back1, back2, back3)
    rows = x_ref.shape[1]
    for step in range(N_Y // 2):
        here = (2 * step, 2 * step + 1)
        out_grad = jnp.concatenate([x_ref[y ^ s, :, :depth] for s in here], axis=0)
        att_grad_all = dot_nt(out_grad, weight_ref[...]).astype(BF16)
        attended, query_grad = [], []
        for pair in range(2):
            columns = slice(depth + pair * PAIR, depth + (pair + 1) * PAIR)
            query = jnp.concatenate([x_ref[y ^ s, :, columns] for s in here], axis=0)
            att_grad = att_grad_all[:, pair * PAIR : (pair + 1) * PAIR]
            scores = dot_nt(key_ref[pair], query)
            prob_grad = dot_nt(value_ref[pair], att_grad)
            probs_low, score_grad = [], []
            for head in range(2):
                part = scores[head * WIDTH : (head + 1) * WIDTH]
                grad = prob_grad[head * WIDTH : (head + 1) * WIDTH]
                top = jnp.max(part, axis=0, keepdims=True)
                expo = jnp.exp((part - top) * SCALE)
                probs = expo * (1.0 / jnp.sum(expo, axis=0, keepdims=True))
                center = jnp.sum(probs * grad, axis=0, keepdims=True)
                probs_low.append(probs.astype(BF16))
                score_grad.append((SCALE * probs * (grad - center)).astype(BF16))
            probs_low = jnp.concatenate(probs_low, axis=0)
            score_grad = jnp.concatenate(score_grad, axis=0)
            attended.append(dot(value_t_ref[pair], probs_low).astype(BF16))
            query_grad.append(dot(key_t_ref[pair], score_grad).astype(BF16))
            key_part = dot(score_grad, query)
            value_part = dot(probs_low, att_grad)
            if step == 0:
                key_acc[pair] = key_part
                value_acc[pair] = value_part
            else:
                key_acc[pair] += key_part
                value_acc[pair] += value_part
        attended = jnp.concatenate(attended, axis=0)
        query_grad = jnp.concatenate(query_grad, axis=0).T
        out_part = dot(attended.T, weight_ref[...]).astype(BF16)
        for k, i in enumerate(here):
            backs[i][:, :depth] = out_part[k * rows : (k + 1) * rows]
            backs[i][:, depth:] = query_grad[k * rows : (k + 1) * rows]
        tile_part = dot(attended, out_grad)
        if step == 0:
            tile_acc[...] = tile_part
        else:
            tile_acc[...] += tile_part
    core = blk_ref[0] & 1
    rows_tile = depth // 2
    for half in range(2):
        turned = tile_acc[half * PAIR : (half + 1) * PAIR, :].T.reshape(-1, 2, chunk, PAIR)
        for to in range(2):
            four_ref[2 * to + half, :rows_tile, :] = turned[:, to].reshape(rows_tile, PAIR).astype(BF16)
        for other in range(2):
            to = 2 * (core ^ other) + half
            for slot in range(WIN // 2 + 1):
                w = 2 * slot + other
                for part, acc in enumerate((key_acc, value_acc)):
                    at = pl.ds(rows_tile + (2 * slot + part) * SRC_DEV, SRC_DEV)
                    if w >= WIN:
                        four_ref[to, at, :] = zero
                        continue
                    first = acc[half, w * SRC_DEV : (w + 1) * SRC_DEV, :]
                    second = acc[half, WIDTH + w * SRC_DEV : WIDTH + (w + 1) * SRC_DEV, :]
                    four_ref[to, at, :] = jnp.where(lane < HD, first, second).astype(BF16)


def attend(tgt, blk, n_blk, x, kvs, mine, theirs):
    _, rows, wide = x.shape
    depth = mine.shape[1]
    flops = 2 * N_Y * rows * (6 * 2 * WIDTH * QUAD + 3 * depth * QUAD)
    return pl.pallas_call(
        functools.partial(attend_kernel, depth // n_blk),
        out_shape=(struct((rows, wide)),) * N_Y
        + (struct((4, depth // 2 + 2 * (WIN // 2 + 1) * SRC_DEV, PAIR)),),
        in_specs=[SMEM] * 2 + [VMEM] * 9,
        out_specs=(VMEM,) * (N_Y + 1),
        scratch_shapes=[
            pltpu.VMEM((2, 2 * WIDTH, PAIR), BF16),
            pltpu.VMEM((2, 2 * WIDTH, PAIR), BF16),
            pltpu.VMEM((2, PAIR, 2 * WIDTH), BF16),
            pltpu.VMEM((2, PAIR, 2 * WIDTH), BF16),
            pltpu.VMEM((QUAD, depth), BF16),
            pltpu.VMEM((2, 2 * WIDTH, PAIR), F32),
            pltpu.VMEM((2, 2 * WIDTH, PAIR), F32),
            pltpu.VMEM((QUAD, depth), F32),
        ],
        cost_estimate=pl.CostEstimate(
            flops=flops, bytes_accessed=4 * N_Y * rows * wide, transcendentals=4 * WIDTH * N_Y * rows
        ),
        compiler_params=pltpu.CompilerParams(vmem_limit_bytes=60 * 1024 * 1024),
        name="attend",
    )(tgt, blk, x, *kvs, mine, theirs)


def combine_kernel(blk_ref, four_ref, tile_ref, own_ref, near_ref, far_ref):
    chips, chunk, _ = tile_ref.shape
    rows_tile = chips * chunk
    block = 2 * SRC_DEV
    core = blk_ref[0] & 1
    total = four_ref[0, :rows_tile, :].astype(F32)
    for i in range(1, 4):
        total = total + four_ref[i, :rows_tile, :].astype(F32)
    tile_ref[...] = total.astype(BF16).reshape(chips, chunk, PAIR)

    def part(of_core, slot):
        at = pl.ds(rows_tile + slot * block, block)
        return four_ref[2 * of_core, at, :].astype(F32) + four_ref[2 * of_core + 1, at, :].astype(F32)

    one, three = part(1 - core, 0), part(1 - core, 1)
    zero = jnp.zeros_like(one)
    first = core == 0
    own_ref[...] = part(core, 0) + jnp.where(first, one, zero)
    near_ref[...] = (part(core, 1) + jnp.where(first, three, one)).astype(BF16)
    far_ref[...] = (part(core, 2) + jnp.where(first, zero, three)).astype(BF16)


def combine(blk, n_blk, four):
    rows_tile = four.shape[1] - 2 * (WIN // 2 + 1) * SRC_DEV
    chips = n_blk // 2
    block = (2 * SRC_DEV, PAIR)
    return pl.pallas_call(
        combine_kernel,
        out_shape=(struct((chips, rows_tile // chips, PAIR)), struct(block, F32), struct(block), struct(block)),
        in_specs=[SMEM, VMEM],
        out_specs=(VMEM,) * 4,
        compiler_params=pltpu.CompilerParams(vmem_limit_bytes=8 * 1024 * 1024),
        name="combine",
    )(blk, four)


def finish_kernel(tgt_ref, back0, back1, back2, back3, own_ref, near_ref, far_ref, out_ref, query_grad_ref, key_grad_ref, value_grad_ref):
    depth = out_ref.shape[1]
    total = None
    for s, ref in enumerate((back0, back1, back2, back3)):
        part = ref[:, :depth].astype(F32)
        total = part if total is None else total + part
        query_grad_ref[:, pl.ds(pl.multiple_of(((tgt_ref[0] >> 1) ^ s) * QUAD, QUAD), QUAD)] = ref[:, depth:]
    out_ref[...] = total.astype(BF16)
    grad = (own_ref[...] + near_ref[...].astype(F32) + far_ref[...].astype(F32)).astype(BF16)
    key_grad_ref[...] = grad[:SRC_DEV]
    value_grad_ref[...] = grad[SRC_DEV:]


def finish(tgt, backs, own, near, far):
    rows, wide = backs[0].shape
    out, grad = struct((rows, wide - QUAD)), struct((SRC_DEV, PAIR))
    return pl.pallas_call(
        finish_kernel,
        out_shape=(out, out, grad, grad),
        in_specs=[SMEM] + [VMEM] * (N_Y + 3),
        out_specs=(VMEM,) * 4,
        cost_estimate=pl.CostEstimate(
            flops=N_Y * rows * wide, bytes_accessed=2 * N_Y * rows * wide, transcendentals=0
        ),
        compiler_params=pltpu.CompilerParams(vmem_limit_bytes=8 * 1024 * 1024),
        name="finish",
    )(tgt, *backs, own, near, far)


def total_kernel(part_ref, total_ref):
    total = part_ref[0].astype(F32)
    for i in range(1, part_ref.shape[0]):
        total = total + part_ref[i].astype(F32)
    total_ref[...] = total.astype(BF16)


def total_of(parts):
    return pl.pallas_call(
        total_kernel,
        out_shape=struct(parts.shape[1:]),
        in_specs=[VMEM],
        out_specs=VMEM,
        compiler_params=pltpu.CompilerParams(vmem_limit_bytes=4 * 1024 * 1024),
        name="total",
    )(parts)


def shift(value, axis, steps):
    count = lax.axis_size(axis)
    return lax.ppermute(value, axis, [(i, (i + steps) % count) for i in range(count)])


def flip(value, bits, blk_bits=0):
    n_tgt = lax.axis_size("tgt")
    devices = range(lax.axis_size("blk") * n_tgt)
    return lax.ppermute(value, ("blk", "tgt"), [(i, i ^ (blk_bits * n_tgt + bits)) for i in devices])


def fetch(value):
    n_tgt, n_blk = lax.axis_size("tgt"), lax.axis_size("blk")
    pairs = [
        (b * n_tgt + t, (b + 2 + 2 * (t & 1)) % n_blk * n_tgt + t) for b in range(n_blk) for t in range(n_tgt)
    ]
    return lax.ppermute(value, ("blk", "tgt"), pairs)


def local(queries, keys, values, out_weight, out_grad):
    n_blk = lax.axis_size("blk")
    n_tgt = lax.axis_size("tgt")
    tgt = lax.axis_index("tgt").reshape(1)
    blk = lax.axis_index("blk").reshape(1)
    own, send = pack(tgt, queries, keys, values, out_grad)
    groups = [[2 * y + low for y in range(N_Y)] for low in range(2)]
    x = lax.all_to_all(
        send, "tgt", split_axis=0, concat_axis=0, tiled=True, axis_index_groups=groups
    )
    kept = fetch(own)
    theirs = flip(out_weight, 1)
    mate = flip(own, 0, 1)
    kvs = [own, mate, kept, flip(kept, 1), flip(kept, 0, 1), flip(kept, 1, 1)]
    *backs, four = attend(tgt, blk, n_blk, x, kvs, out_weight, theirs)
    fours = [
        [(2 * chip + core) * n_tgt + 2 * y + low for core in range(2) for low in range(2)]
        for chip in range(n_blk // 2)
        for y in range(N_Y)
    ]
    four = lax.all_to_all(four, ("blk", "tgt"), split_axis=0, concat_axis=0, tiled=True, axis_index_groups=fours)
    backs = [backs[0]] + [flip(backs[s], 2 * s) for s in range(1, N_Y)]
    tile, own_grad, near, far = combine(blk, n_blk, four)
    cores = [list(range(core, n_blk, 2)) for core in range(2)]
    tiles = lax.all_to_all(
        tile, "blk", split_axis=0, concat_axis=0, tiled=True, axis_index_groups=cores
    )
    near, far = shift(near, "blk", -2), shift(far, "blk", -4)
    outputs, query_grad, key_grad, value_grad = finish(tgt, backs, own_grad, near, far)
    weight_grad = total_of(tiles).T
    return outputs, query_grad, key_grad, value_grad, weight_grad


def solution(mesh):
    return jax.shard_map(
        local,
        mesh=mesh,
        in_specs=(
            P(("blk", "tgt"), None),
            P("blk", None),
            P("blk", None),
            P("tgt", None),
            P(("blk", "tgt"), None),
        ),
        out_specs=(
            P(("blk", "tgt"), None),
            P(("blk", "tgt"), None),
            P("blk", "tgt"),
            P("blk", "tgt"),
            P("tgt", "blk"),
        ),
        check_vma=False,
    )
```

```python
import functools

import jax
import jax.numpy as jnp
from jax import lax
from jax.experimental import pallas as pl
from jax.experimental.pallas import tpu as pltpu
from jax.sharding import PartitionSpec as P


HD = 64
PAIR = 2 * HD
QUAD = 2 * PAIR
WIN = 5
SRC_DEV = 64
WIDTH = WIN * SRC_DEV
SCALE = HD ** -0.5
N_Y = 4
F32 = jnp.float32
BF16 = jnp.bfloat16
NT = (((1,), (1,)), ((), ()))
VMEM = pl.BlockSpec(memory_space=pltpu.VMEM)
SMEM = pl.BlockSpec(memory_space=pltpu.SMEM)


def dot(a, b):
    return jnp.dot(a, b, preferred_element_type=F32)


def dot_nt(a, b):
    return lax.dot_general(a, b, NT, preferred_element_type=F32)


def struct(shape, dtype=BF16):
    return jax.ShapeDtypeStruct(shape, dtype)


def pack_kernel(tgt_ref, query_ref, key_ref, value_ref, out_grad_ref, own_ref, send_ref, grad_buf, query_buf, block_buf, sems):
    depth = grad_buf.shape[1]
    mine = pl.ds(pl.multiple_of((tgt_ref[0] >> 1) * QUAD, QUAD), QUAD)
    ins = [
        pltpu.make_async_copy(out_grad_ref, grad_buf, sems.at[0]),
        pltpu.make_async_copy(query_ref, query_buf, sems.at[1]),
        pltpu.make_async_copy(key_ref.at[:, mine], block_buf.at[:, :QUAD], sems.at[2]),
        pltpu.make_async_copy(value_ref.at[:, mine], block_buf.at[:, QUAD:], sems.at[3]),
    ]
    for copy in ins:
        copy.start()
    ins[0].wait()
    outs = [pltpu.make_async_copy(grad_buf, send_ref.at[i, :, :depth], sems.at[4 + i]) for i in range(N_Y)]
    for copy in outs:
        copy.start()
    ins[1].wait()
    more = [
        pltpu.make_async_copy(query_buf.at[:, i * QUAD : (i + 1) * QUAD], send_ref.at[i, :, depth:], sems.at[8 + i])
        for i in range(N_Y)
    ]
    for copy in more:
        copy.start()
    ins[2].wait()
    ins[3].wait()
    last = pltpu.make_async_copy(block_buf, own_ref, sems.at[12])
    last.start()
    for copy in outs + more + [last]:
        copy.wait()


def pack(tgt, queries, keys, values, out_grad):
    rows, depth = queries.shape
    anywhere = pl.BlockSpec(memory_space=pl.ANY)
    return pl.pallas_call(
        pack_kernel,
        out_shape=(struct((SRC_DEV, 2 * QUAD)), struct((N_Y, rows, depth + QUAD))),
        in_specs=[SMEM] + [anywhere] * 4,
        out_specs=(anywhere,) * 2,
        scratch_shapes=[
            pltpu.VMEM((rows, depth), BF16),
            pltpu.VMEM((rows, depth), BF16),
            pltpu.VMEM((SRC_DEV, 2 * QUAD), BF16),
            pltpu.SemaphoreType.DMA((13,)),
        ],
        compiler_params=pltpu.CompilerParams(vmem_limit_bytes=60 * 1024 * 1024),
        name="pack",
    )(tgt, queries, keys, values, out_grad)


def attend_kernel(
    chunk, tgt_ref, blk_ref, x_ref, own_ref, kv1_ref, kv2_ref, kv3_ref, kv4_ref, mine_ref, theirs_ref,
    back0, back1, back2, back3, four_ref,
    key_ref, value_ref, key_t_ref, value_t_ref, weight_ref, key_acc, value_acc, tile_acc,
):
    depth = mine_ref.shape[1]
    y = tgt_ref[0] >> 1
    low = tgt_ref[0] & 1
    lane = lax.broadcasted_iota(jnp.int32, (SRC_DEV, PAIR), 1)
    zero = jnp.zeros((SRC_DEV, PAIR), BF16)
    weight_ref[pl.ds(pl.multiple_of(low * PAIR, PAIR), PAIR), :] = mine_ref[...]
    weight_ref[pl.ds(pl.multiple_of((1 - low) * PAIR, PAIR), PAIR), :] = theirs_ref[...]
    for pair in range(2):
        for w, ref in enumerate((own_ref, kv1_ref, kv2_ref, kv3_ref, kv4_ref)):
            block_key = ref[:, pair * PAIR : (pair + 1) * PAIR]
            block_value = ref[:, QUAD + pair * PAIR : QUAD + (pair + 1) * PAIR]
            for head in range(2):
                own_lanes = (lane < HD) if head == 0 else (lane >= HD)
                at = pl.ds(head * WIDTH + w * SRC_DEV, SRC_DEV)
                key_ref[pair, at, :] = jnp.where(own_lanes, block_key, zero)
                value_ref[pair, at, :] = jnp.where(own_lanes, block_value, zero)
        key_t_ref[pair] = key_ref[pair].T
        value_t_ref[pair] = value_ref[pair].T
    backs = (back0, back1, back2, back3)
    rows = x_ref.shape[1]
    for step in range(N_Y // 2):
        here = (2 * step, 2 * step + 1)
        out_grad = jnp.concatenate([x_ref[y ^ s, :, :depth] for s in here], axis=0)
        att_grad_all = dot_nt(out_grad, weight_ref[...]).astype(BF16)
        attended, query_grad = [], []
        for pair in range(2):
            columns = slice(depth + pair * PAIR, depth + (pair + 1) * PAIR)
            query = jnp.concatenate([x_ref[y ^ s, :, columns] for s in here], axis=0)
            att_grad = att_grad_all[:, pair * PAIR : (pair + 1) * PAIR]
            scores = dot_nt(key_ref[pair], query)
            prob_grad = dot_nt(value_ref[pair], att_grad)
            probs_low, score_grad = [], []
            for head in range(2):
                part = scores[head * WIDTH : (head + 1) * WIDTH]
                grad = prob_grad[head * WIDTH : (head + 1) * WIDTH]
                top = jnp.max(part, axis=0, keepdims=True)
                expo = jnp.exp((part - top) * SCALE)
                probs = expo * (1.0 / jnp.sum(expo, axis=0, keepdims=True))
                center = jnp.sum(probs * grad, axis=0, keepdims=True)
                probs_low.append(probs.astype(BF16))
                score_grad.append((SCALE * probs * (grad - center)).astype(BF16))
            probs_low = jnp.concatenate(probs_low, axis=0)
            score_grad = jnp.concatenate(score_grad, axis=0)
            attended.append(dot(value_t_ref[pair], probs_low).astype(BF16))
            query_grad.append(dot(key_t_ref[pair], score_grad).astype(BF16))
            key_part = dot(score_grad, query)
            value_part = dot(probs_low, att_grad)
            if step == 0:
                key_acc[pair] = key_part
                value_acc[pair] = value_part
            else:
                key_acc[pair] += key_part
                value_acc[pair] += value_part
        attended = jnp.concatenate(attended, axis=0)
        query_grad = jnp.concatenate(query_grad, axis=0).T
        out_part = dot(attended.T, weight_ref[...]).astype(BF16)
        for k, i in enumerate(here):
            backs[i][:, :depth] = out_part[k * rows : (k + 1) * rows]
            backs[i][:, depth:] = query_grad[k * rows : (k + 1) * rows]
        tile_part = dot(attended, out_grad)
        if step == 0:
            tile_acc[...] = tile_part
        else:
            tile_acc[...] += tile_part
    core = blk_ref[0] & 1
    rows_tile = depth // 2
    for half in range(2):
        turned = tile_acc[half * PAIR : (half + 1) * PAIR, :].T.reshape(-1, 2, chunk, PAIR)
        for to in range(2):
            four_ref[2 * to + half, :rows_tile, :] = turned[:, to].reshape(rows_tile, PAIR).astype(BF16)
        for other in range(2):
            to = 2 * (core ^ other) + half
            for slot in range(WIN // 2 + 1):
                w = 2 * slot + other
                for part, acc in enumerate((key_acc, value_acc)):
                    at = pl.ds(rows_tile + (2 * slot + part) * SRC_DEV, SRC_DEV)
                    if w >= WIN:
                        four_ref[to, at, :] = zero
                        continue
                    first = acc[half, w * SRC_DEV : (w + 1) * SRC_DEV, :]
                    second = acc[half, WIDTH + w * SRC_DEV : WIDTH + (w + 1) * SRC_DEV, :]
                    four_ref[to, at, :] = jnp.where(lane < HD, first, second).astype(BF16)


def attend(tgt, blk, n_blk, x, kvs, mine, theirs):
    _, rows, wide = x.shape
    depth = mine.shape[1]
    flops = 2 * N_Y * rows * (6 * 2 * WIDTH * QUAD + 3 * depth * QUAD)
    return pl.pallas_call(
        functools.partial(attend_kernel, depth // n_blk),
        out_shape=(struct((rows, wide)),) * N_Y
        + (struct((4, depth // 2 + 2 * (WIN // 2 + 1) * SRC_DEV, PAIR)),),
        in_specs=[SMEM] * 2 + [VMEM] * 8,
        out_specs=(VMEM,) * (N_Y + 1),
        scratch_shapes=[
            pltpu.VMEM((2, 2 * WIDTH, PAIR), BF16),
            pltpu.VMEM((2, 2 * WIDTH, PAIR), BF16),
            pltpu.VMEM((2, PAIR, 2 * WIDTH), BF16),
            pltpu.VMEM((2, PAIR, 2 * WIDTH), BF16),
            pltpu.VMEM((QUAD, depth), BF16),
            pltpu.VMEM((2, 2 * WIDTH, PAIR), F32),
            pltpu.VMEM((2, 2 * WIDTH, PAIR), F32),
            pltpu.VMEM((QUAD, depth), F32),
        ],
        cost_estimate=pl.CostEstimate(
            flops=flops, bytes_accessed=4 * N_Y * rows * wide, transcendentals=4 * WIDTH * N_Y * rows
        ),
        compiler_params=pltpu.CompilerParams(vmem_limit_bytes=32 * 1024 * 1024),
        name="attend",
    )(tgt, blk, x, *kvs, mine, theirs)


def combine_kernel(blk_ref, four_ref, tile_ref, own_ref, near_ref, far_ref):
    chips, chunk, _ = tile_ref.shape
    rows_tile = chips * chunk
    block = 2 * SRC_DEV
    core = blk_ref[0] & 1
    total = four_ref[0, :rows_tile, :].astype(F32)
    for i in range(1, 4):
        total = total + four_ref[i, :rows_tile, :].astype(F32)
    tile_ref[...] = total.astype(BF16).reshape(chips, chunk, PAIR)

    def part(of_core, slot):
        at = pl.ds(rows_tile + slot * block, block)
        return four_ref[2 * of_core, at, :].astype(F32) + four_ref[2 * of_core + 1, at, :].astype(F32)

    one, three = part(1 - core, 0), part(1 - core, 1)
    zero = jnp.zeros_like(one)
    first = core == 0
    own_ref[...] = part(core, 0) + jnp.where(first, one, zero)
    near_ref[...] = (part(core, 1) + jnp.where(first, three, one)).astype(BF16)
    far_ref[...] = (part(core, 2) + jnp.where(first, zero, three)).astype(BF16)


def combine(blk, n_blk, four):
    rows_tile = four.shape[1] - 2 * (WIN // 2 + 1) * SRC_DEV
    chips = n_blk // 2
    block = (2 * SRC_DEV, PAIR)
    return pl.pallas_call(
        combine_kernel,
        out_shape=(struct((chips, rows_tile // chips, PAIR)), struct(block, F32), struct(block), struct(block)),
        in_specs=[SMEM, VMEM],
        out_specs=(VMEM,) * 4,
        compiler_params=pltpu.CompilerParams(vmem_limit_bytes=8 * 1024 * 1024),
        name="combine",
    )(blk, four)


def finish_kernel(tgt_ref, back0, back1, back2, back3, own_ref, near_ref, far_ref, out_ref, query_grad_ref, key_grad_ref, value_grad_ref):
    depth = out_ref.shape[1]
    total = None
    for s, ref in enumerate((back0, back1, back2, back3)):
        part = ref[:, :depth].astype(F32)
        total = part if total is None else total + part
        query_grad_ref[:, pl.ds(pl.multiple_of(((tgt_ref[0] >> 1) ^ s) * QUAD, QUAD), QUAD)] = ref[:, depth:]
    out_ref[...] = total.astype(BF16)
    grad = (own_ref[...] + near_ref[...].astype(F32) + far_ref[...].astype(F32)).astype(BF16)
    key_grad_ref[...] = grad[:SRC_DEV]
    value_grad_ref[...] = grad[SRC_DEV:]


def finish(tgt, backs, own, near, far):
    rows, wide = backs[0].shape
    out, grad = struct((rows, wide - QUAD)), struct((SRC_DEV, PAIR))
    return pl.pallas_call(
        finish_kernel,
        out_shape=(out, out, grad, grad),
        in_specs=[SMEM] + [VMEM] * (N_Y + 3),
        out_specs=(VMEM,) * 4,
        cost_estimate=pl.CostEstimate(
            flops=N_Y * rows * wide, bytes_accessed=2 * N_Y * rows * wide, transcendentals=0
        ),
        compiler_params=pltpu.CompilerParams(vmem_limit_bytes=8 * 1024 * 1024),
        name="finish",
    )(tgt, *backs, own, near, far)


def total_kernel(part_ref, total_ref):
    total = part_ref[0].astype(F32)
    for i in range(1, part_ref.shape[0]):
        total = total + part_ref[i].astype(F32)
    total_ref[...] = total.astype(BF16)


def total_of(parts):
    return pl.pallas_call(
        total_kernel,
        out_shape=struct(parts.shape[1:]),
        in_specs=[VMEM],
        out_specs=VMEM,
        compiler_params=pltpu.CompilerParams(vmem_limit_bytes=4 * 1024 * 1024),
        name="total",
    )(parts)


def shift(value, axis, steps):
    count = lax.axis_size(axis)
    return lax.ppermute(value, axis, [(i, (i + steps) % count) for i in range(count)])


def flip(value, bits):
    return lax.ppermute(value, "tgt", [(i, i ^ bits) for i in range(lax.axis_size("tgt"))])


def local(queries, keys, values, out_weight, out_grad):
    n_blk = lax.axis_size("blk")
    n_tgt = lax.axis_size("tgt")
    tgt = lax.axis_index("tgt").reshape(1)
    blk = lax.axis_index("blk").reshape(1)
    own, send = pack(tgt, queries, keys, values, out_grad)
    groups = [[2 * y + low for y in range(N_Y)] for low in range(2)]
    x = lax.all_to_all(
        send, "tgt", split_axis=0, concat_axis=0, tiled=True, axis_index_groups=groups
    )
    theirs = flip(out_weight, 1)
    kvs = [own] + [shift(own, "blk", w) for w in range(1, WIN)]
    *backs, four = attend(tgt, blk, n_blk, x, kvs, out_weight, theirs)
    fours = [
        [(2 * chip + core) * n_tgt + 2 * y + low for core in range(2) for low in range(2)]
        for chip in range(n_blk // 2)
        for y in range(N_Y)
    ]
    four = lax.all_to_all(four, ("blk", "tgt"), split_axis=0, concat_axis=0, tiled=True, axis_index_groups=fours)
    backs = [backs[0]] + [flip(backs[s], 2 * s) for s in range(1, N_Y)]
    tile, own_grad, near, far = combine(blk, n_blk, four)
    cores = [list(range(core, n_blk, 2)) for core in range(2)]
    tiles = lax.all_to_all(
        tile, "blk", split_axis=0, concat_axis=0, tiled=True, axis_index_groups=cores
    )
    near, far = shift(near, "blk", -2), shift(far, "blk", -4)
    outputs, query_grad, key_grad, value_grad = finish(tgt, backs, own_grad, near, far)
    weight_grad = total_of(tiles).T
    return outputs, query_grad, key_grad, value_grad, weight_grad


def solution(mesh):
    return jax.shard_map(
        local,
        mesh=mesh,
        in_specs=(
            P(("blk", "tgt"), None),
            P("blk", None),
            P("blk", None),
            P("tgt", None),
            P(("blk", "tgt"), None),
        ),
        out_specs=(
            P(("blk", "tgt"), None),
            P(("blk", "tgt"), None),
            P("blk", "tgt"),
            P("blk", "tgt"),
            P("tgt", "blk"),
        ),
        check_vma=False,
    )
```

```python
import functools

import jax
import jax.numpy as jnp
from jax import lax
from jax.experimental import pallas as pl
from jax.experimental.pallas import tpu as pltpu
from jax.sharding import PartitionSpec as P


HD = 64
PAIR = 2 * HD
QUAD = 2 * PAIR
WIN = 5
SRC_DEV = 64
WIDTH = WIN * SRC_DEV
SCALE = HD ** -0.5
N_Y = 4
F32 = jnp.float32
BF16 = jnp.bfloat16
NT = (((1,), (1,)), ((), ()))
VMEM = pl.BlockSpec(memory_space=pltpu.VMEM)
SMEM = pl.BlockSpec(memory_space=pltpu.SMEM)


def dot(a, b):
    return jnp.dot(a, b, preferred_element_type=F32)


def dot_nt(a, b):
    return lax.dot_general(a, b, NT, preferred_element_type=F32)


def struct(shape, dtype=BF16):
    return jax.ShapeDtypeStruct(shape, dtype)


def pack_kernel(tgt_ref, query_ref, key_ref, value_ref, out_grad_ref, own_ref, send_ref, grad_buf, query_buf, block_buf, sems):
    depth = grad_buf.shape[1]
    mine = pl.ds(pl.multiple_of((tgt_ref[0] >> 1) * QUAD, QUAD), QUAD)
    ins = [
        pltpu.make_async_copy(out_grad_ref, grad_buf, sems.at[0]),
        pltpu.make_async_copy(query_ref, query_buf, sems.at[1]),
        pltpu.make_async_copy(key_ref.at[:, mine], block_buf.at[:, :QUAD], sems.at[2]),
        pltpu.make_async_copy(value_ref.at[:, mine], block_buf.at[:, QUAD:], sems.at[3]),
    ]
    for copy in ins:
        copy.start()
    ins[0].wait()
    outs = [pltpu.make_async_copy(grad_buf, send_ref.at[i, :, :depth], sems.at[4 + i]) for i in range(N_Y)]
    for copy in outs:
        copy.start()
    ins[1].wait()
    more = [
        pltpu.make_async_copy(query_buf.at[:, i * QUAD : (i + 1) * QUAD], send_ref.at[i, :, depth:], sems.at[8 + i])
        for i in range(N_Y)
    ]
    for copy in more:
        copy.start()
    ins[2].wait()
    ins[3].wait()
    last = pltpu.make_async_copy(block_buf, own_ref, sems.at[12])
    last.start()
    for copy in outs + more + [last]:
        copy.wait()


def pack(tgt, queries, keys, values, out_grad):
    rows, depth = queries.shape
    anywhere = pl.BlockSpec(memory_space=pl.ANY)
    return pl.pallas_call(
        pack_kernel,
        out_shape=(struct((SRC_DEV, 2 * QUAD)), struct((N_Y, rows, depth + QUAD))),
        in_specs=[SMEM] + [anywhere] * 4,
        out_specs=(anywhere,) * 2,
        scratch_shapes=[
            pltpu.VMEM((rows, depth), BF16),
            pltpu.VMEM((rows, depth), BF16),
            pltpu.VMEM((SRC_DEV, 2 * QUAD), BF16),
            pltpu.SemaphoreType.DMA((13,)),
        ],
        compiler_params=pltpu.CompilerParams(vmem_limit_bytes=60 * 1024 * 1024),
        name="pack",
    )(tgt, queries, keys, values, out_grad)


def attend_kernel(
    chunk, tgt_ref, blk_ref, x_ref, own_ref, near_ref, far_ref, mate_own_ref, mate_near_ref, mate_far_ref, mine_ref, theirs_ref,
    back0, back1, back2, back3, four_ref,
    key_ref, value_ref, key_t_ref, value_t_ref, weight_ref, key_acc, value_acc, tile_acc,
):
    depth = mine_ref.shape[1]
    y = tgt_ref[0] >> 1
    low = tgt_ref[0] & 1
    lane = lax.broadcasted_iota(jnp.int32, (SRC_DEV, PAIR), 1)
    zero = jnp.zeros((SRC_DEV, PAIR), BF16)
    weight_ref[pl.ds(pl.multiple_of(low * PAIR, PAIR), PAIR), :] = mine_ref[...]
    weight_ref[pl.ds(pl.multiple_of((1 - low) * PAIR, PAIR), PAIR), :] = theirs_ref[...]
    first = (blk_ref[0] & 1) == 0
    mate_near = mate_near_ref[...]
    blocks = (
        own_ref[...],
        jnp.where(first, mate_near, mate_own_ref[...]),
        near_ref[...],
        jnp.where(first, mate_far_ref[...], mate_near),
        far_ref[...],
    )
    for pair in range(2):
        for w, block in enumerate(blocks):
            block_key = block[:, pair * PAIR : (pair + 1) * PAIR]
            block_value = block[:, QUAD + pair * PAIR : QUAD + (pair + 1) * PAIR]
            for head in range(2):
                own_lanes = (lane < HD) if head == 0 else (lane >= HD)
                at = pl.ds(head * WIDTH + w * SRC_DEV, SRC_DEV)
                key_ref[pair, at, :] = jnp.where(own_lanes, block_key, zero)
                value_ref[pair, at, :] = jnp.where(own_lanes, block_value, zero)
        key_t_ref[pair] = key_ref[pair].T
        value_t_ref[pair] = value_ref[pair].T
    backs = (back0, back1, back2, back3)
    rows = x_ref.shape[1]
    for step in range(N_Y // 2):
        here = (2 * step, 2 * step + 1)
        out_grad = jnp.concatenate([x_ref[y ^ s, :, :depth] for s in here], axis=0)
        att_grad_all = dot_nt(out_grad, weight_ref[...]).astype(BF16)
        attended, query_grad = [], []
        for pair in range(2):
            columns = slice(depth + pair * PAIR, depth + (pair + 1) * PAIR)
            query = jnp.concatenate([x_ref[y ^ s, :, columns] for s in here], axis=0)
            att_grad = att_grad_all[:, pair * PAIR : (pair + 1) * PAIR]
            scores = dot_nt(key_ref[pair], query)
            prob_grad = dot_nt(value_ref[pair], att_grad)
            probs_low, score_grad = [], []
            for head in range(2):
                part = scores[head * WIDTH : (head + 1) * WIDTH]
                grad = prob_grad[head * WIDTH : (head + 1) * WIDTH]
                top = jnp.max(part, axis=0, keepdims=True)
                expo = jnp.exp((part - top) * SCALE)
                probs = expo * (1.0 / jnp.sum(expo, axis=0, keepdims=True))
                center = jnp.sum(probs * grad, axis=0, keepdims=True)
                probs_low.append(probs.astype(BF16))
                score_grad.append((SCALE * probs * (grad - center)).astype(BF16))
            probs_low = jnp.concatenate(probs_low, axis=0)
            score_grad = jnp.concatenate(score_grad, axis=0)
            attended.append(dot(value_t_ref[pair], probs_low).astype(BF16))
            query_grad.append(dot(key_t_ref[pair], score_grad).astype(BF16))
            key_part = dot(score_grad, query)
            value_part = dot(probs_low, att_grad)
            if step == 0:
                key_acc[pair] = key_part
                value_acc[pair] = value_part
            else:
                key_acc[pair] += key_part
                value_acc[pair] += value_part
        attended = jnp.concatenate(attended, axis=0)
        query_grad = jnp.concatenate(query_grad, axis=0).T
        out_part = dot(attended.T, weight_ref[...]).astype(BF16)
        for k, i in enumerate(here):
            backs[i][:, :depth] = out_part[k * rows : (k + 1) * rows]
            backs[i][:, depth:] = query_grad[k * rows : (k + 1) * rows]
        tile_part = dot(attended, out_grad)
        if step == 0:
            tile_acc[...] = tile_part
        else:
            tile_acc[...] += tile_part
    core = blk_ref[0] & 1
    rows_tile = depth // 2
    for half in range(2):
        turned = tile_acc[half * PAIR : (half + 1) * PAIR, :].T.reshape(-1, 2, chunk, PAIR)
        for to in range(2):
            four_ref[2 * to + half, :rows_tile, :] = turned[:, to].reshape(rows_tile, PAIR).astype(BF16)
        for other in range(2):
            to = 2 * (core ^ other) + half
            for slot in range(WIN // 2 + 1):
                w = 2 * slot + other
                for part, acc in enumerate((key_acc, value_acc)):
                    at = pl.ds(rows_tile + (2 * slot + part) * SRC_DEV, SRC_DEV)
                    if w >= WIN:
                        four_ref[to, at, :] = zero
                        continue
                    first = acc[half, w * SRC_DEV : (w + 1) * SRC_DEV, :]
                    second = acc[half, WIDTH + w * SRC_DEV : WIDTH + (w + 1) * SRC_DEV, :]
                    four_ref[to, at, :] = jnp.where(lane < HD, first, second).astype(BF16)


def attend(tgt, blk, n_blk, x, kvs, mine, theirs):
    _, rows, wide = x.shape
    depth = mine.shape[1]
    flops = 2 * N_Y * rows * (6 * 2 * WIDTH * QUAD + 3 * depth * QUAD)
    return pl.pallas_call(
        functools.partial(attend_kernel, depth // n_blk),
        out_shape=(struct((rows, wide)),) * N_Y
        + (struct((4, depth // 2 + 2 * (WIN // 2 + 1) * SRC_DEV, PAIR)),),
        in_specs=[SMEM] * 2 + [VMEM] * 9,
        out_specs=(VMEM,) * (N_Y + 1),
        scratch_shapes=[
            pltpu.VMEM((2, 2 * WIDTH, PAIR), BF16),
            pltpu.VMEM((2, 2 * WIDTH, PAIR), BF16),
            pltpu.VMEM((2, PAIR, 2 * WIDTH), BF16),
            pltpu.VMEM((2, PAIR, 2 * WIDTH), BF16),
            pltpu.VMEM((QUAD, depth), BF16),
            pltpu.VMEM((2, 2 * WIDTH, PAIR), F32),
            pltpu.VMEM((2, 2 * WIDTH, PAIR), F32),
            pltpu.VMEM((QUAD, depth), F32),
        ],
        cost_estimate=pl.CostEstimate(
            flops=flops, bytes_accessed=4 * N_Y * rows * wide, transcendentals=4 * WIDTH * N_Y * rows
        ),
        compiler_params=pltpu.CompilerParams(vmem_limit_bytes=32 * 1024 * 1024),
        name="attend",
    )(tgt, blk, x, *kvs, mine, theirs)


def combine_kernel(blk_ref, four_ref, tile_ref, own_ref, near_ref, far_ref):
    chips, chunk, _ = tile_ref.shape
    rows_tile = chips * chunk
    block = 2 * SRC_DEV
    core = blk_ref[0] & 1
    total = four_ref[0, :rows_tile, :].astype(F32)
    for i in range(1, 4):
        total = total + four_ref[i, :rows_tile, :].astype(F32)
    tile_ref[...] = total.astype(BF16).reshape(chips, chunk, PAIR)

    def part(of_core, slot):
        at = pl.ds(rows_tile + slot * block, block)
        return four_ref[2 * of_core, at, :].astype(F32) + four_ref[2 * of_core + 1, at, :].astype(F32)

    one, three = part(1 - core, 0), part(1 - core, 1)
    zero = jnp.zeros_like(one)
    first = core == 0
    own_ref[...] = part(core, 0) + jnp.where(first, one, zero)
    near_ref[...] = (part(core, 1) + jnp.where(first, three, one)).astype(BF16)
    far_ref[...] = (part(core, 2) + jnp.where(first, zero, three)).astype(BF16)


def combine(blk, n_blk, four):
    rows_tile = four.shape[1] - 2 * (WIN // 2 + 1) * SRC_DEV
    chips = n_blk // 2
    block = (2 * SRC_DEV, PAIR)
    return pl.pallas_call(
        combine_kernel,
        out_shape=(struct((chips, rows_tile // chips, PAIR)), struct(block, F32), struct(block), struct(block)),
        in_specs=[SMEM, VMEM],
        out_specs=(VMEM,) * 4,
        compiler_params=pltpu.CompilerParams(vmem_limit_bytes=8 * 1024 * 1024),
        name="combine",
    )(blk, four)


def finish_kernel(tgt_ref, back0, back1, back2, back3, own_ref, near_ref, far_ref, out_ref, query_grad_ref, key_grad_ref, value_grad_ref):
    depth = out_ref.shape[1]
    total = None
    for s, ref in enumerate((back0, back1, back2, back3)):
        part = ref[:, :depth].astype(F32)
        total = part if total is None else total + part
        query_grad_ref[:, pl.ds(pl.multiple_of(((tgt_ref[0] >> 1) ^ s) * QUAD, QUAD), QUAD)] = ref[:, depth:]
    out_ref[...] = total.astype(BF16)
    grad = (own_ref[...] + near_ref[...].astype(F32) + far_ref[...].astype(F32)).astype(BF16)
    key_grad_ref[...] = grad[:SRC_DEV]
    value_grad_ref[...] = grad[SRC_DEV:]


def finish(tgt, backs, own, near, far):
    rows, wide = backs[0].shape
    out, grad = struct((rows, wide - QUAD)), struct((SRC_DEV, PAIR))
    return pl.pallas_call(
        finish_kernel,
        out_shape=(out, out, grad, grad),
        in_specs=[SMEM] + [VMEM] * (N_Y + 3),
        out_specs=(VMEM,) * 4,
        cost_estimate=pl.CostEstimate(
            flops=N_Y * rows * wide, bytes_accessed=2 * N_Y * rows * wide, transcendentals=0
        ),
        compiler_params=pltpu.CompilerParams(vmem_limit_bytes=8 * 1024 * 1024),
        name="finish",
    )(tgt, *backs, own, near, far)


def total_kernel(part_ref, total_ref):
    total = part_ref[0].astype(F32)
    for i in range(1, part_ref.shape[0]):
        total = total + part_ref[i].astype(F32)
    total_ref[...] = total.astype(BF16)


def total_of(parts):
    return pl.pallas_call(
        total_kernel,
        out_shape=struct(parts.shape[1:]),
        in_specs=[VMEM],
        out_specs=VMEM,
        compiler_params=pltpu.CompilerParams(vmem_limit_bytes=4 * 1024 * 1024),
        name="total",
    )(parts)


def shift(value, axis, steps):
    count = lax.axis_size(axis)
    return lax.ppermute(value, axis, [(i, (i + steps) % count) for i in range(count)])


def mate(value):
    return lax.ppermute(value, "blk", [(i, i ^ 1) for i in range(lax.axis_size("blk"))])


def flip(value, bits):
    return lax.ppermute(value, "tgt", [(i, i ^ bits) for i in range(lax.axis_size("tgt"))])


def local(queries, keys, values, out_weight, out_grad):
    n_blk = lax.axis_size("blk")
    n_tgt = lax.axis_size("tgt")
    tgt = lax.axis_index("tgt").reshape(1)
    blk = lax.axis_index("blk").reshape(1)
    own, send = pack(tgt, queries, keys, values, out_grad)
    groups = [[2 * y + low for y in range(N_Y)] for low in range(2)]
    x = lax.all_to_all(
        send, "tgt", split_axis=0, concat_axis=0, tiled=True, axis_index_groups=groups
    )
    theirs = flip(out_weight, 1)
    near = shift(own, "blk", 2)
    far = shift(own, "blk", 4)
    mate_own = mate(own)
    kvs = [own, near, far, mate_own, mate(near), mate(far)]
    *backs, four = attend(tgt, blk, n_blk, x, kvs, out_weight, theirs)
    fours = [
        [(2 * chip + core) * n_tgt + 2 * y + low for core in range(2) for low in range(2)]
        for chip in range(n_blk // 2)
        for y in range(N_Y)
    ]
    four = lax.all_to_all(four, ("blk", "tgt"), split_axis=0, concat_axis=0, tiled=True, axis_index_groups=fours)
    backs = [backs[0]] + [flip(backs[s], 2 * s) for s in range(1, N_Y)]
    tile, own_grad, near, far = combine(blk, n_blk, four)
    cores = [list(range(core, n_blk, 2)) for core in range(2)]
    tiles = lax.all_to_all(
        tile, "blk", split_axis=0, concat_axis=0, tiled=True, axis_index_groups=cores
    )
    near, far = shift(near, "blk", -2), shift(far, "blk", -4)
    outputs, query_grad, key_grad, value_grad = finish(tgt, backs, own_grad, near, far)
    weight_grad = total_of(tiles).T
    return outputs, query_grad, key_grad, value_grad, weight_grad


def solution(mesh):
    return jax.shard_map(
        local,
        mesh=mesh,
        in_specs=(
            P(("blk", "tgt"), None),
            P("blk", None),
            P("blk", None),
            P("tgt", None),
            P(("blk", "tgt"), None),
        ),
        out_specs=(
            P(("blk", "tgt"), None),
            P(("blk", "tgt"), None),
            P("blk", "tgt"),
            P("blk", "tgt"),
            P("tgt", "blk"),
        ),
        check_vma=False,
    )
```

```python
import functools

import jax
import jax.numpy as jnp
from jax import lax
from jax.experimental import pallas as pl
from jax.experimental.pallas import tpu as pltpu
from jax.sharding import PartitionSpec as P


HD = 64
PAIR = 2 * HD
QUAD = 2 * PAIR
WIN = 5
SRC_DEV = 64
WIDTH = WIN * SRC_DEV
SCALE = HD ** -0.5
N_Y = 4
F32 = jnp.float32
BF16 = jnp.bfloat16
NT = (((1,), (1,)), ((), ()))
VMEM = pl.BlockSpec(memory_space=pltpu.VMEM)
SMEM = pl.BlockSpec(memory_space=pltpu.SMEM)


def dot(a, b):
    return jnp.dot(a, b, preferred_element_type=F32)


def dot_nt(a, b):
    return lax.dot_general(a, b, NT, preferred_element_type=F32)


def struct(shape, dtype=BF16):
    return jax.ShapeDtypeStruct(shape, dtype)


def pack_kernel(tgt_ref, query_ref, key_ref, value_ref, out_grad_ref, own_ref, send_ref, grad_buf, query_buf, block_buf, sems):
    depth = grad_buf.shape[1]
    mine = pl.ds(pl.multiple_of((tgt_ref[0] >> 1) * QUAD, QUAD), QUAD)
    ins = [
        pltpu.make_async_copy(out_grad_ref, grad_buf, sems.at[0]),
        pltpu.make_async_copy(query_ref, query_buf, sems.at[1]),
        pltpu.make_async_copy(key_ref.at[:, mine], block_buf.at[:, :QUAD], sems.at[2]),
        pltpu.make_async_copy(value_ref.at[:, mine], block_buf.at[:, QUAD:], sems.at[3]),
    ]
    for copy in ins:
        copy.start()
    ins[0].wait()
    outs = [pltpu.make_async_copy(grad_buf, send_ref.at[i, :, :depth], sems.at[4 + i]) for i in range(N_Y)]
    for copy in outs:
        copy.start()
    ins[1].wait()
    more = [
        pltpu.make_async_copy(query_buf.at[:, i * QUAD : (i + 1) * QUAD], send_ref.at[i, :, depth:], sems.at[8 + i])
        for i in range(N_Y)
    ]
    for copy in more:
        copy.start()
    ins[2].wait()
    ins[3].wait()
    last = pltpu.make_async_copy(block_buf, own_ref, sems.at[12])
    last.start()
    for copy in outs + more + [last]:
        copy.wait()


def pack(tgt, queries, keys, values, out_grad):
    rows, depth = queries.shape
    anywhere = pl.BlockSpec(memory_space=pl.ANY)
    return pl.pallas_call(
        pack_kernel,
        out_shape=(struct((SRC_DEV, 2 * QUAD)), struct((N_Y, rows, depth + QUAD))),
        in_specs=[SMEM] + [anywhere] * 4,
        out_specs=(anywhere,) * 2,
        scratch_shapes=[
            pltpu.VMEM((rows, depth), BF16),
            pltpu.VMEM((rows, depth), BF16),
            pltpu.VMEM((SRC_DEV, 2 * QUAD), BF16),
            pltpu.SemaphoreType.DMA((13,)),
        ],
        compiler_params=pltpu.CompilerParams(vmem_limit_bytes=60 * 1024 * 1024),
        name="pack",
    )(tgt, queries, keys, values, out_grad)


def attend_kernel(
    chunk, tgt_ref, blk_ref, x_ref, own_ref, kv1_ref, kv2_ref, kv3_ref, kv4_ref, mine_ref, theirs_ref,
    back0, back1, back2, back3, four_ref, own_keep_ref, own_send_ref,
    key_ref, value_ref, key_t_ref, value_t_ref, weight_ref, key_acc, value_acc, tile_acc,
):
    depth = mine_ref.shape[1]
    y = tgt_ref[0] >> 1
    low = tgt_ref[0] & 1
    lane = lax.broadcasted_iota(jnp.int32, (SRC_DEV, PAIR), 1)
    zero = jnp.zeros((SRC_DEV, PAIR), BF16)
    weight_ref[pl.ds(pl.multiple_of(low * PAIR, PAIR), PAIR), :] = mine_ref[...]
    weight_ref[pl.ds(pl.multiple_of((1 - low) * PAIR, PAIR), PAIR), :] = theirs_ref[...]
    for pair in range(2):
        for w, ref in enumerate((own_ref, kv1_ref, kv2_ref, kv3_ref, kv4_ref)):
            block_key = ref[:, pair * PAIR : (pair + 1) * PAIR]
            block_value = ref[:, QUAD + pair * PAIR : QUAD + (pair + 1) * PAIR]
            for head in range(2):
                own_lanes = (lane < HD) if head == 0 else (lane >= HD)
                at = pl.ds(head * WIDTH + w * SRC_DEV, SRC_DEV)
                key_ref[pair, at, :] = jnp.where(own_lanes, block_key, zero)
                value_ref[pair, at, :] = jnp.where(own_lanes, block_value, zero)
        key_t_ref[pair] = key_ref[pair].T
        value_t_ref[pair] = value_ref[pair].T
    backs = (back0, back1, back2, back3)
    rows = x_ref.shape[1]
    for step in range(N_Y // 2):
        here = (2 * step, 2 * step + 1)
        out_grad = jnp.concatenate([x_ref[y ^ s, :, :depth] for s in here], axis=0)
        att_grad_all = dot_nt(out_grad, weight_ref[...]).astype(BF16)
        attended, query_grad = [], []
        for pair in range(2):
            columns = slice(depth + pair * PAIR, depth + (pair + 1) * PAIR)
            query = jnp.concatenate([x_ref[y ^ s, :, columns] for s in here], axis=0)
            att_grad = att_grad_all[:, pair * PAIR : (pair + 1) * PAIR]
            scores = dot_nt(key_ref[pair], query)
            prob_grad = dot_nt(value_ref[pair], att_grad)
            probs_low, score_grad = [], []
            for head in range(2):
                part = scores[head * WIDTH : (head + 1) * WIDTH]
                grad = prob_grad[head * WIDTH : (head + 1) * WIDTH]
                top = jnp.max(part, axis=0, keepdims=True)
                expo = jnp.exp((part - top) * SCALE)
                probs = expo * (1.0 / jnp.sum(expo, axis=0, keepdims=True))
                center = jnp.sum(probs * grad, axis=0, keepdims=True)
                probs_low.append(probs.astype(BF16))
                score_grad.append((SCALE * probs * (grad - center)).astype(BF16))
            probs_low = jnp.concatenate(probs_low, axis=0)
            score_grad = jnp.concatenate(score_grad, axis=0)
            attended.append(dot(value_t_ref[pair], probs_low).astype(BF16))
            query_grad.append(dot(key_t_ref[pair], score_grad).astype(BF16))
            key_part = dot(score_grad, query)
            value_part = dot(probs_low, att_grad)
            if step == 0:
                key_acc[pair] = key_part
                value_acc[pair] = value_part
            else:
                key_acc[pair] += key_part
                value_acc[pair] += value_part
        attended = jnp.concatenate(attended, axis=0)
        query_grad = jnp.concatenate(query_grad, axis=0).T
        out_part = dot(attended.T, weight_ref[...]).astype(BF16)
        for k, i in enumerate(here):
            backs[i][:, :depth] = out_part[k * rows : (k + 1) * rows]
            backs[i][:, depth:] = query_grad[k * rows : (k + 1) * rows]
        tile_part = dot(attended, out_grad)
        if step == 0:
            tile_acc[...] = tile_part
        else:
            tile_acc[...] += tile_part
    core = blk_ref[0] & 1
    rows_tile = depth // 2
    for half in range(2):
        turned = tile_acc[half * PAIR : (half + 1) * PAIR, :].T.reshape(-1, 2, chunk, PAIR)
        for to in range(2):
            four_ref[2 * to + half, :rows_tile, :] = turned[:, to].reshape(rows_tile, PAIR).astype(BF16)
        for other in range(2):
            to = 2 * (core ^ other) + half
            for slot in range(WIN // 2):
                w = 2 * slot + 2 - other
                for part, acc in enumerate((key_acc, value_acc)):
                    at = pl.ds(rows_tile + (2 * slot + part) * SRC_DEV, SRC_DEV)
                    first_head = acc[half, w * SRC_DEV : (w + 1) * SRC_DEV, :]
                    second_head = acc[half, WIDTH + w * SRC_DEV : WIDTH + (w + 1) * SRC_DEV, :]
                    four_ref[to, at, :] = jnp.where(lane < HD, first_head, second_head).astype(BF16)
    for pair, ref in ((low, own_keep_ref), (1 - low, own_send_ref)):
        for part, acc in enumerate((key_acc, value_acc)):
            first_head = acc[pair, :SRC_DEV, :]
            second_head = acc[pair, WIDTH : WIDTH + SRC_DEV, :]
            at = slice(part * SRC_DEV, (part + 1) * SRC_DEV)
            ref[at, :] = jnp.where(lane < HD, first_head, second_head).astype(ref.dtype)


def attend(tgt, blk, n_blk, x, kvs, mine, theirs):
    _, rows, wide = x.shape
    depth = mine.shape[1]
    flops = 2 * N_Y * rows * (6 * 2 * WIDTH * QUAD + 3 * depth * QUAD)
    return pl.pallas_call(
        functools.partial(attend_kernel, depth // n_blk),
        out_shape=(struct((rows, wide)),) * N_Y
        + (
            struct((4, depth // 2 + 2 * (WIN // 2) * SRC_DEV, PAIR)),
            struct((2 * SRC_DEV, PAIR), F32),
            struct((2 * SRC_DEV, PAIR)),
        ),
        in_specs=[SMEM] * 2 + [VMEM] * 8,
        out_specs=(VMEM,) * (N_Y + 3),
        scratch_shapes=[
            pltpu.VMEM((2, 2 * WIDTH, PAIR), BF16),
            pltpu.VMEM((2, 2 * WIDTH, PAIR), BF16),
            pltpu.VMEM((2, PAIR, 2 * WIDTH), BF16),
            pltpu.VMEM((2, PAIR, 2 * WIDTH), BF16),
            pltpu.VMEM((QUAD, depth), BF16),
            pltpu.VMEM((2, 2 * WIDTH, PAIR), F32),
            pltpu.VMEM((2, 2 * WIDTH, PAIR), F32),
            pltpu.VMEM((QUAD, depth), F32),
        ],
        cost_estimate=pl.CostEstimate(
            flops=flops, bytes_accessed=4 * N_Y * rows * wide, transcendentals=4 * WIDTH * N_Y * rows
        ),
        compiler_params=pltpu.CompilerParams(vmem_limit_bytes=32 * 1024 * 1024),
        name="attend",
    )(tgt, blk, x, *kvs, mine, theirs)


def combine_kernel(blk_ref, four_ref, tile_ref, own_ref, near_ref, far_ref):
    chips, chunk, _ = tile_ref.shape
    rows_tile = chips * chunk
    block = 2 * SRC_DEV
    core = blk_ref[0] & 1
    total = four_ref[0, :rows_tile, :].astype(F32)
    for i in range(1, 4):
        total = total + four_ref[i, :rows_tile, :].astype(F32)
    tile_ref[...] = total.astype(BF16).reshape(chips, chunk, PAIR)

    def part(of_core, slot):
        at = pl.ds(rows_tile + slot * block, block)
        return four_ref[2 * of_core, at, :].astype(F32) + four_ref[2 * of_core + 1, at, :].astype(F32)

    one, three = part(1 - core, 0), part(1 - core, 1)
    zero = jnp.zeros_like(one)
    first = core == 0
    own_ref[...] = jnp.where(first, one, zero)
    near_ref[...] = (part(core, 0) + jnp.where(first, three, one)).astype(BF16)
    far_ref[...] = (part(core, 1) + jnp.where(first, zero, three)).astype(BF16)


def combine(blk, n_blk, four):
    rows_tile = four.shape[1] - 2 * (WIN // 2) * SRC_DEV
    chips = n_blk // 2
    block = (2 * SRC_DEV, PAIR)
    return pl.pallas_call(
        combine_kernel,
        out_shape=(struct((chips, rows_tile // chips, PAIR)), struct(block, F32), struct(block), struct(block)),
        in_specs=[SMEM, VMEM],
        out_specs=(VMEM,) * 4,
        compiler_params=pltpu.CompilerParams(vmem_limit_bytes=8 * 1024 * 1024),
        name="combine",
    )(blk, four)


def finish_kernel(tgt_ref, back0, back1, back2, back3, own_ref, keep_ref, came_ref, near_ref, far_ref, out_ref, query_grad_ref, key_grad_ref, value_grad_ref):
    depth = out_ref.shape[1]
    total = None
    for s, ref in enumerate((back0, back1, back2, back3)):
        part = ref[:, :depth].astype(F32)
        total = part if total is None else total + part
        query_grad_ref[:, pl.ds(pl.multiple_of(((tgt_ref[0] >> 1) ^ s) * QUAD, QUAD), QUAD)] = ref[:, depth:]
    out_ref[...] = total.astype(BF16)
    grad = own_ref[...] + keep_ref[...]
    for ref in (came_ref, near_ref, far_ref):
        grad = grad + ref[...].astype(F32)
    grad = grad.astype(BF16)
    key_grad_ref[...] = grad[:SRC_DEV]
    value_grad_ref[...] = grad[SRC_DEV:]


def finish(tgt, backs, *grads):
    rows, wide = backs[0].shape
    out, grad = struct((rows, wide - QUAD)), struct((SRC_DEV, PAIR))
    return pl.pallas_call(
        finish_kernel,
        out_shape=(out, out, grad, grad),
        in_specs=[SMEM] + [VMEM] * (N_Y + 5),
        out_specs=(VMEM,) * 4,
        cost_estimate=pl.CostEstimate(
            flops=N_Y * rows * wide, bytes_accessed=2 * N_Y * rows * wide, transcendentals=0
        ),
        compiler_params=pltpu.CompilerParams(vmem_limit_bytes=8 * 1024 * 1024),
        name="finish",
    )(tgt, *backs, *grads)


def total_kernel(part_ref, total_ref):
    total = part_ref[0].astype(F32)
    for i in range(1, part_ref.shape[0]):
        total = total + part_ref[i].astype(F32)
    total_ref[...] = total.astype(BF16)


def total_of(parts):
    return pl.pallas_call(
        total_kernel,
        out_shape=struct(parts.shape[1:]),
        in_specs=[VMEM],
        out_specs=VMEM,
        compiler_params=pltpu.CompilerParams(vmem_limit_bytes=4 * 1024 * 1024),
        name="total",
    )(parts)


def shift(value, axis, steps):
    count = lax.axis_size(axis)
    return lax.ppermute(value, axis, [(i, (i + steps) % count) for i in range(count)])


def flip(value, bits):
    return lax.ppermute(value, "tgt", [(i, i ^ bits) for i in range(lax.axis_size("tgt"))])


def local(queries, keys, values, out_weight, out_grad):
    n_blk = lax.axis_size("blk")
    n_tgt = lax.axis_size("tgt")
    tgt = lax.axis_index("tgt").reshape(1)
    blk = lax.axis_index("blk").reshape(1)
    own, send = pack(tgt, queries, keys, values, out_grad)
    groups = [[2 * y + low for y in range(N_Y)] for low in range(2)]
    x = lax.all_to_all(
        send, "tgt", split_axis=0, concat_axis=0, tiled=True, axis_index_groups=groups
    )
    theirs = flip(out_weight, 1)
    kvs = [own] + [shift(own, "blk", w) for w in range(1, WIN)]
    *backs, four, own_keep, own_send = attend(tgt, blk, n_blk, x, kvs, out_weight, theirs)
    fours = [
        [(2 * chip + core) * n_tgt + 2 * y + low for core in range(2) for low in range(2)]
        for chip in range(n_blk // 2)
        for y in range(N_Y)
    ]
    four = lax.all_to_all(four, ("blk", "tgt"), split_axis=0, concat_axis=0, tiled=True, axis_index_groups=fours)
    backs = [backs[0]] + [flip(backs[s], 2 * s) for s in range(1, N_Y)]
    tile, own_grad, near, far = combine(blk, n_blk, four)
    cores = [list(range(core, n_blk, 2)) for core in range(2)]
    tiles = lax.all_to_all(
        tile, "blk", split_axis=0, concat_axis=0, tiled=True, axis_index_groups=cores
    )
    near, far = shift(near, "blk", -2), shift(far, "blk", -4)
    came = flip(own_send, 1)
    outputs, query_grad, key_grad, value_grad = finish(tgt, backs, own_grad, own_keep, came, near, far)
    weight_grad = total_of(tiles).T
    return outputs, query_grad, key_grad, value_grad, weight_grad


def solution(mesh):
    return jax.shard_map(
        local,
        mesh=mesh,
        in_specs=(
            P(("blk", "tgt"), None),
            P("blk", None),
            P("blk", None),
            P("tgt", None),
            P(("blk", "tgt"), None),
        ),
        out_specs=(
            P(("blk", "tgt"), None),
            P(("blk", "tgt"), None),
            P("blk", "tgt"),
            P("blk", "tgt"),
            P("tgt", "blk"),
        ),
        check_vma=False,
    )
```
